256 devices in a mesh: blk: 64 (over y_lo, z, x), rep: 4 (over y_hi, core).
Axes of the slice: x: 4, y: 4 (y_hi: 2, y_lo: 2; y = y_hi * 2 + y_lo), z: 8, core: 2. Of those that a mesh axis runs over, the one named last changes fastest.
Arguments:
- features: bfloat16 [262144, 128], P(('blk', 'rep')), may hold values from -6 to 6
- weight: bfloat16 [128, 512], replicated, may hold values from -0.5 to 0.5
- bias: float32 [512], replicated, may hold values from -3 to 3
- tile_values: bfloat16 [262144, 4096], P(('blk', 'rep')), may hold values from -0.125 to 0.125
- tile_cols: int32 [2048, 32], P(('blk', 'rep')), may hold values from 0 to 95, as said below
- tile_counts: int32 [2048], P(('blk', 'rep')), may hold values from 1 to 32, as said below
- out_grad: bfloat16 [262144, 512], P(('blk', 'rep')), may hold values from -6 to 6
Outputs:
- activations: bfloat16 [262144, 512], P(('blk', 'rep'))
- feature_grad: float32 [262144, 128], P(('blk', 'rep'))
- weight_grad: float32 [128, 512], replicated
- bias_grad: float32 [512], replicated
The draws below stay inside these ranges and needn't reach their ends.
Inputs may be any that keep to these rules, and one draw needn't show every extreme that they name: `tile_cols`: within one row tile the 32 entries are different. `tile_counts`: slots 0 to count - 1 of a row tile are live.
All inputs are finite; a program needn't handle non-finite values.
Results may differ from the reference program's by a relative error of at most 0.0059.
Values may be sent and summed in bfloat16 or wider, within the bound.
No kernel may reach another device: no remote copies, remote signals or barrier semaphores. Data moves between devices by JAX's collectives and lax.ppermute only.
A program may use at most 128 MiB of HBM per device.

```python
import jax
import jax.numpy as jnp
from jax import lax

IN_DIM = 128
OUT_DIM = 512
TILE = 128
REACH = 1
SLOTS = 32
NODES = 262144
BLK_TILES = 32
ROW_TILES = 2048
N_BLK = 64


def draw_tile_cols(key, part):
    window_tiles = (2 * REACH + 1) * BLK_TILES
    subkeys = jax.random.split(jax.random.fold_in(key, 11), ROW_TILES)
    chosen = jax.vmap(lambda subkey: jax.random.permutation(subkey, window_tiles)[:SLOTS])(subkeys)
    return chosen.astype(jnp.int32)


def draw_tile_counts(key, part):
    counts = jax.random.randint(jax.random.fold_in(key, 21), (ROW_TILES,), 1, SLOTS + 1)
    fullest = jax.random.randint(jax.random.fold_in(key, 22), (), 0, ROW_TILES)
    return jnp.where(jnp.arange(ROW_TILES) == fullest, SLOTS, counts).astype(jnp.int32)


def levels(own_key, shape, pieces, smallest, largest):
    def one(dim, shards_of):
        heights = jax.random.uniform(jax.random.fold_in(jax.random.fold_in(own_key, 6), dim), (shards_of,), jnp.float32, smallest / len(pieces), largest / len(pieces))
        return jnp.repeat(jnp.exp(heights), shape[dim] // shards_of).reshape((-1,) + (1,) * (len(shape) - dim - 1))

    factor_of = one(*pieces[0])
    for cut in pieces[1:]:
        factor_of = factor_of * one(*cut)
    return factor_of


def scatter_about(own_key, extent, deviation, reach, shards=(), kind=jnp.bfloat16):
    array = deviation * jax.random.normal(own_key, extent, jnp.float32)
    if shards:
        array = array * levels(own_key, extent, shards, -0.22, 0.18)
    return jnp.clip(array, -reach, reach).astype(kind)


def setup_inputs(seed: int = 0) -> dict:
    key_of = jax.random.split(jax.random.key(seed), 8)
    features = scatter_about(key_of[0], (NODES, IN_DIM), 1.0, 6.0, ((0, 256),))
    weight = scatter_about(key_of[1], (IN_DIM, OUT_DIM), IN_DIM ** -0.5, 0.5)
    bias = scatter_about(key_of[2], (OUT_DIM,), 0.5, 3.0, (), jnp.float32)
    tile_values = scatter_about(key_of[3], (NODES, SLOTS * TILE), (SLOTS * TILE // 2) ** -0.5, 0.125, ((0, 256),))
    tile_cols = draw_tile_cols(jax.random.fold_in(key_of[7], 71), 0)
    tile_counts = draw_tile_counts(jax.random.fold_in(key_of[7], 71), 0)
    out_grad = scatter_about(key_of[6], (NODES, OUT_DIM), 1.0, 6.0, ((0, 256),))
    return dict(features=features, weight=weight, bias=bias, tile_values=tile_values, tile_cols=tile_cols, tile_counts=tile_counts, out_grad=out_grad)


def gelu_parts(pre_act):
    inner = 0.7978845608028654 * (pre_act + 0.044715 * pre_act * pre_act * pre_act)
    tangent = jnp.tanh(inner)
    value_part = 0.5 * pre_act * (1.0 + tangent)
    slope = 0.5 * (1.0 + tangent) + 0.5 * pre_act * (1.0 - tangent * tangent) * 0.7978845608028654 * (1.0 + 0.134145 * pre_act * pre_act)
    return value_part, slope


def reference(features, weight, bias, tile_values, tile_cols, tile_counts, out_grad):
    row_ids = jnp.arange(ROW_TILES).astype(jnp.int32)
    row_block = (row_ids // BLK_TILES).astype(jnp.int32)
    block_offset = (tile_cols // BLK_TILES - REACH).astype(jnp.int32)
    col_block = ((row_block[:, None] + block_offset + N_BLK) % N_BLK).astype(jnp.int32)
    global_tile = (col_block * BLK_TILES + tile_cols % BLK_TILES).astype(jnp.int32)
    is_live = jnp.arange(SLOTS).astype(jnp.int32)[None, :] < tile_counts[:, None]
    feature_tiles = features.reshape(ROW_TILES, TILE, IN_DIM)
    value_tiles = tile_values.reshape(ROW_TILES, TILE, SLOTS * TILE)

    def forward_tile(packed):
        tile_block, targets, alive = packed
        gathered = feature_tiles[targets]
        gathered = jnp.where(alive[:, None, None], gathered, jnp.zeros((), gathered.dtype))
        return jnp.dot(tile_block, gathered.reshape(SLOTS * TILE, IN_DIM), preferred_element_type=jnp.float32)

    summed = lax.map(forward_tile, (value_tiles, global_tile, is_live))
    aggregated = summed.reshape(NODES, IN_DIM).astype(jnp.bfloat16)
    pre_act = jnp.dot(aggregated, weight, preferred_element_type=jnp.float32) + bias
    value_part, slope = gelu_parts(pre_act)
    activations = value_part.astype(jnp.bfloat16)
    pre_grad = (out_grad.astype(jnp.float32) * slope).astype(jnp.bfloat16)
    factor = NODES ** -0.5
    weight_grad = jnp.dot(aggregated.T, pre_grad, preferred_element_type=jnp.float32) * factor
    bias_grad = jnp.sum(pre_grad.astype(jnp.float32), axis=0) * factor
    row_grad = jnp.dot(pre_grad, weight.T, preferred_element_type=jnp.float32).astype(jnp.bfloat16)
    grad_tiles = row_grad.reshape(ROW_TILES, TILE, IN_DIM)

    def backward_tile(running, packed):
        tile_block, targets, alive, grad_rows = packed
        partial_value = jnp.dot(tile_block.T, grad_rows, preferred_element_type=jnp.float32).reshape(SLOTS, TILE, IN_DIM)
        partial_value = jnp.where(alive[:, None, None], partial_value, jnp.zeros((), partial_value.dtype))
        return running.at[targets].add(partial_value), None

    initial = jnp.zeros((ROW_TILES, TILE, IN_DIM), jnp.float32)
    feature_grad, unused = lax.scan(backward_tile, initial, (value_tiles, global_tile, is_live, grad_tiles))
    return (activations, feature_grad.reshape(NODES, IN_DIM), weight_grad, bias_grad)
```

```python
import functools
import math

import jax
import jax.numpy as jnp
from jax import lax
from jax.experimental import pallas as pl
from jax.experimental.pallas import tpu as pltpu
from jax.sharding import PartitionSpec as P

TILE = 128
REACH = 1
SLOTS = 32
GROUP = 4
PIECE_TILES = 8
PIECES = (2 * REACH + 1) * GROUP
DUMMY = PIECES * PIECE_TILES
AXES = ("blk", "rep")


def sent(value, target):
    count = lax.axis_size("blk") * lax.axis_size("rep")
    return lax.ppermute(value, AXES, [(source, target(source, count)) for source in range(count)])


def to_core(value):
    return sent(value, lambda device, count: device ^ 1)


def to_row(value):
    return sent(value, lambda device, count: device ^ 2)


def to_block(value, steps):
    return sent(value, lambda device, count: (device + GROUP * steps) % count)


def to_block_bit(value, bit):
    return sent(value, lambda device, count: device ^ (GROUP << bit))


def gelu_parts(pre_act):
    inner = 0.7978845608028654 * (pre_act + 0.044715 * pre_act * pre_act * pre_act)
    tangent = jnp.tanh(inner)
    value_part = 0.5 * pre_act * (1.0 + tangent)
    slope = 0.5 * (1.0 + tangent) + 0.5 * pre_act * (
        1.0 - tangent * tangent
    ) * 0.7978845608028654 * (1.0 + 0.134145 * pre_act * pre_act)
    return (value_part, slope)


def forward_kernel(
    factor, place_ref, rep_ref, window_ref, values_ref, grad_ref, weight_ref, bias_ref,
    act_ref, back_ref, sums_ref, agg_ref, pre_ref, bias_sum_ref,
):
    step = pl.program_id(0)
    total = None
    for pair in range(SLOTS // 2):
        one = window_ref[place_ref[step, 2 * pair]]
        two = window_ref[place_ref[step, 2 * pair + 1]]
        term = jnp.dot(
            values_ref[:, 2 * pair * TILE : (2 * pair + 2) * TILE],
            jnp.concatenate([one, two], axis=0),
            preferred_element_type=jnp.float32,
        )
        total = term if total is None else total + term
    aggregated = total.astype(jnp.bfloat16)
    weight = weight_ref[...]
    pre_act = jnp.dot(aggregated, weight, preferred_element_type=jnp.float32) + bias_ref[...]
    value_part, slope = gelu_parts(pre_act)
    act_ref[...] = value_part.astype(jnp.bfloat16)
    pre_wide = (grad_ref[...].astype(jnp.float32) * slope).astype(jnp.bfloat16)
    back_ref[...] = lax.dot_general(
        weight, pre_wide, (((1,), (1,)), ((), ())), preferred_element_type=jnp.float32
    ).astype(jnp.bfloat16)
    rows = pl.ds(pl.multiple_of(step * TILE, TILE), TILE)
    agg_ref[rows, :] = aggregated
    pre_ref[rows, :] = pre_wide
    part = jnp.sum(pre_wide.astype(jnp.float32).reshape(TILE // 8, 8, -1), axis=0)

    @pl.when(step == 0)
    def _():
        bias_sum_ref[...] = part

    @pl.when(step > 0)
    def _():
        bias_sum_ref[...] += part

    @pl.when(step == pl.num_programs(0) - 1)
    def _():
        sums = factor * lax.dot_general(
            agg_ref[...], pre_ref[...], (((0,), (0,)), ((), ())), preferred_element_type=jnp.float32
        )
        rep = rep_ref[0]
        rows_of = TILE // GROUP
        for chunk in range(GROUP):
            turn = jnp.bitwise_xor(rep, chunk)
            spot = (turn & 1) * 2 + (turn >> 1)
            sums_ref[spot, :rows_of, :] = sums[chunk * rows_of : (chunk + 1) * rows_of]
            sums_ref[spot, rows_of:, :] = bias_sum_ref[...] * factor


def backward_kernel(place_ref, back_ref, values_ref, keep_ref, send_ref, total_ref):
    step = pl.program_id(0)

    @pl.when(step == 0)
    def _():
        total_ref[...] = jnp.zeros_like(total_ref)

    back = back_ref[...]
    for pair in range(SLOTS // 2):
        term = jnp.dot(
            back,
            values_ref[:, 2 * pair * TILE : (2 * pair + 2) * TILE],
            preferred_element_type=jnp.float32,
        )
        for half in range(2):
            spot = place_ref[step, 2 * pair + half]
            total_ref[spot] += term[:, half * TILE : (half + 1) * TILE]

    @pl.when(step == pl.num_programs(0) - 1)
    def _():
        half = DUMMY // 2
        keep_ref[...] = total_ref[:half].astype(jnp.bfloat16)
        send_ref[...] = total_ref[half : 2 * half].astype(jnp.bfloat16)


def on_device(features, weight, bias, tile_values, tile_cols, tile_counts, out_grad):
    rows_dev, in_dim = features.shape
    out_dim = weight.shape[1]
    row_tiles = rows_dev // TILE
    nodes = rows_dev * lax.axis_size("rep") * lax.axis_size("blk")
    factor = 1.0 / math.sqrt(nodes)
    rep = lax.axis_index("rep")

    other_row = to_row(features)
    pieces = {0: (features, other_row)}
    for steps in (1, -1):
        pieces[-steps] = (to_block(features, steps), to_block(other_row, steps))
    near = [piece for offset in (-1, 0, 1) for piece in pieces[offset]]
    far = [to_core(piece) for piece in near]
    blank = jnp.zeros_like(features)
    window = jnp.stack(near + far + [blank]).reshape(-1, TILE, in_dim)

    block_tile = tile_cols % (GROUP * PIECE_TILES)
    offset = tile_cols // (GROUP * PIECE_TILES)
    turn = (block_tile // PIECE_TILES) ^ rep
    place = ((turn & 1) * (PIECES // 2) + offset * 2 + (turn >> 1)) * PIECE_TILES
    place = place + block_tile % PIECE_TILES
    is_live = jnp.arange(SLOTS)[None, :] < tile_counts[:, None]
    place = jnp.where(is_live, place, DUMMY).astype(jnp.int32)

    whole = lambda *shape: pl.BlockSpec(shape, lambda i, *_: (0,) * len(shape))
    act, back, sums = pl.pallas_call(
        functools.partial(forward_kernel, factor),
        out_shape=(
            jax.ShapeDtypeStruct((rows_dev, out_dim), jnp.bfloat16),
            jax.ShapeDtypeStruct((in_dim, rows_dev), jnp.bfloat16),
            jax.ShapeDtypeStruct((GROUP, TILE // GROUP + 8, out_dim), jnp.float32),
        ),
        grid_spec=pltpu.PrefetchScalarGridSpec(
            num_scalar_prefetch=2,
            grid=(row_tiles,),
            in_specs=[
                whole(*window.shape),
                pl.BlockSpec((TILE, SLOTS * TILE), lambda i, *_: (i, 0)),
                pl.BlockSpec((TILE, out_dim), lambda i, *_: (i, 0)),
                whole(in_dim, out_dim),
                whole(1, out_dim),
            ],
            out_specs=(
                pl.BlockSpec((TILE, out_dim), lambda i, *_: (i, 0)),
                pl.BlockSpec((in_dim, TILE), lambda i, *_: (0, i)),
                whole(GROUP, TILE // GROUP + 8, out_dim),
            ),
            scratch_shapes=[
                pltpu.VMEM((rows_dev, in_dim), jnp.bfloat16),
                pltpu.VMEM((rows_dev, out_dim), jnp.bfloat16),
                pltpu.VMEM((8, out_dim), jnp.float32),
            ],
        ),
        compiler_params=pltpu.CompilerParams(vmem_limit_bytes=24 << 20),
        cost_estimate=pl.CostEstimate(flops=3 << 30, bytes_accessed=15 << 20, transcendentals=1 << 19),
        name="forward",
    )(place, rep.reshape(1).astype(jnp.int32), window, tile_values, out_grad, weight, bias.reshape(1, -1))

    half_tiles = DUMMY // 2
    keep, send = pl.pallas_call(
        backward_kernel,
        out_shape=(jax.ShapeDtypeStruct((half_tiles, in_dim, TILE), jnp.bfloat16),) * 2,
        grid_spec=pltpu.PrefetchScalarGridSpec(
            num_scalar_prefetch=1,
            grid=(row_tiles,),
            in_specs=[
                pl.BlockSpec((in_dim, TILE), lambda i, *_: (0, i)),
                pl.BlockSpec((TILE, SLOTS * TILE), lambda i, *_: (i, 0)),
            ],
            out_specs=(whole(half_tiles, in_dim, TILE),) * 2,
            scratch_shapes=[pltpu.VMEM((DUMMY + 1, in_dim, TILE), jnp.float32)],
        ),
        compiler_params=pltpu.CompilerParams(vmem_limit_bytes=24 << 20),
        cost_estimate=pl.CostEstimate(flops=2 << 30, bytes_accessed=12 << 20, transcendentals=0),
        name="backward",
    )(place, back, tile_values)

    sums = sums[:2] + to_core(sums[2:])
    mine = sums[0] + to_row(sums[1])
    for bit in range(int(math.log2(lax.axis_size("blk")))):
        mine = mine + to_block_bit(mine, bit)
    bias_grad = jnp.sum(mine[TILE // GROUP :], axis=0)
    mine = mine[: TILE // GROUP]
    theirs = to_row(mine)
    upper, odd = (rep >> 1) == 1, (rep & 1) == 1
    rows = jnp.stack([jnp.where(upper, theirs, mine), jnp.where(upper, mine, theirs)])
    others = to_core(rows)
    weight_grad = jnp.stack([jnp.where(odd, others, rows), jnp.where(odd, rows, others)], axis=1)
    weight_grad = weight_grad.reshape(in_dim, out_dim)

    terms = keep.reshape(3, 2, -1, in_dim, TILE).astype(jnp.float32)
    terms = terms + to_core(send).reshape(terms.shape).astype(jnp.float32)
    block_total = terms[1]
    for steps in (1, -1):
        moved = to_block(terms[1 + steps].astype(jnp.bfloat16), steps)
        block_total = block_total + moved.astype(jnp.float32)
    last = to_row(block_total[1].astype(jnp.bfloat16)).astype(jnp.float32)
    feature_grad = jnp.swapaxes(block_total[0] + last, 1, 2).reshape(rows_dev, in_dim)
    return (act, feature_grad, weight_grad, bias_grad)


def solution(mesh):
    in_specs = (
        P(AXES, None),
        P(),
        P(),
        P(AXES, None),
        P(AXES, None),
        P(AXES),
        P(AXES, None),
    )
    out_specs = (P(AXES, None), P(AXES, None), P(), P())
    return jax.shard_map(
        on_device, mesh=mesh, in_specs=in_specs, out_specs=out_specs, check_vma=False
    )
```

```python
import functools
import math

import jax
import jax.numpy as jnp
from jax import lax
from jax.experimental import pallas as pl
from jax.experimental.pallas import tpu as pltpu
from jax.sharding import PartitionSpec as P


TILE = 128
REACH = 1
SLOTS = 32
GROUP = 4
PIECE_TILES = 8
PIECES = (2 * REACH + 1) * GROUP
DUMMY = PIECES * PIECE_TILES
AXES = ("y_lo", "z", "x", "y_hi", "core")
NEAR = ("x", "y_hi")
FAR = ("y_lo", "z")
VMEM_LIMIT = 32 << 20
SPLIT = (2, 8, 4, 2, 2)
STEP_TILES = 1


def sent(value, target):
    count = lax.axis_size(AXES)
    return lax.ppermute(value, AXES, [(source, target(source, count)) for source in range(count)])


def to_core(value):
    return sent(value, lambda device, count: device ^ 1)


def to_row(value):
    return sent(value, lambda device, count: device ^ 2)


def to_block(value, steps):
    return sent(value, lambda device, count: (device + GROUP * steps) % count)


def to_all(value, axes):
    count = lax.axis_size(axes)
    copies = jnp.broadcast_to(value[None], (count,) + value.shape)
    return lax.all_to_all(copies, axes, 0, 0, tiled=True)


def gelu_parts(pre_act):
    inner = 0.7978845608028654 * (pre_act + 0.044715 * pre_act * pre_act * pre_act)
    tangent = jnp.tanh(inner)
    value_part = 0.5 * pre_act * (1.0 + tangent)
    slope = 0.5 * (1.0 + tangent) + 0.5 * pre_act * (
        1.0 - tangent * tangent
    ) * 0.7978845608028654 * (1.0 + 0.134145 * pre_act * pre_act)
    return (value_part, slope)


def streamed(step, source_ref, held_ref, arrived):
    def copy(tile):
        rows = pl.ds(pl.multiple_of(tile * TILE, TILE), TILE)
        return pltpu.make_async_copy(source_ref.at[rows], held_ref.at[tile], arrived.at[tile])

    @pl.when(step == 0)
    def _():
        for tile in range(held_ref.shape[0]):
            copy(tile).start()

    copy(step).wait()
    return held_ref.at[step]


def forward_kernel(
    factor, place_ref, core_ref, window_ref, source_ref, grad_ref, weight_ref, bias_ref,
    act_ref, back_ref, own_ref, other_ref, agg_ref, pre_ref, bias_sum_ref, held_ref, arrived,
):
    step = pl.program_id(0)
    values_ref = streamed(step, source_ref, held_ref, arrived)
    weight = weight_ref[...]
    for sub in range(STEP_TILES):
        rows = slice(sub * TILE, (sub + 1) * TILE)
        tile = step * STEP_TILES + sub
        total = None
        for pair in range(SLOTS // 2):
            one = window_ref[place_ref[tile, 2 * pair]]
            two = window_ref[place_ref[tile, 2 * pair + 1]]
            term = jnp.dot(
                values_ref[:, 2 * pair * TILE : (2 * pair + 2) * TILE],
                jnp.concatenate([one, two], axis=0),
                preferred_element_type=jnp.float32,
            )
            total = term if total is None else total + term
        aggregated = total.astype(jnp.bfloat16)
        pre_act = jnp.dot(aggregated, weight, preferred_element_type=jnp.float32) + bias_ref[...]
        value_part, slope = gelu_parts(pre_act)
        act_ref[rows, :] = value_part.astype(jnp.bfloat16)
        pre_wide = (grad_ref[rows, :].astype(jnp.float32) * slope).astype(jnp.bfloat16)
        back_ref[:, rows] = lax.dot_general(
            weight, pre_wide, (((1,), (1,)), ((), ())), preferred_element_type=jnp.float32
        ).astype(jnp.bfloat16)
        place = pl.ds(pl.multiple_of(tile * TILE, TILE), TILE)
        agg_ref[place, :] = aggregated
        pre_ref[place, :] = pre_wide
        part = jnp.sum(pre_wide.astype(jnp.float32).reshape(TILE // 8, 8, -1), axis=0)
        bias_sum_ref[pl.ds(pl.multiple_of(tile * 8, 8), 8), :] = part

    @pl.when(step == pl.num_programs(0) - 1)
    def _():
        sums = factor * lax.dot_general(
            agg_ref[...], pre_ref[...], (((0,), (0,)), ((), ())), preferred_element_type=jnp.float32
        )
        bias_sum = jnp.sum(bias_sum_ref[...], axis=0, keepdims=True) * factor
        count, rows_of, _ = own_ref.shape
        out_dim = sums.shape[1]
        parts = [bias_sum[:, i * TILE : (i + 1) * TILE] for i in range(out_dim // TILE)]
        parts.append(jnp.zeros((rows_of - len(parts), TILE), jnp.float32))
        side = jnp.concatenate(parts, axis=0)
        for turn, sums_ref in enumerate((own_ref, other_ref)):
            core = jnp.bitwise_xor(core_ref[0], turn)
            for chunk in range(count):
                low = sums[2 * chunk * rows_of : (2 * chunk + 1) * rows_of]
                high = sums[(2 * chunk + 1) * rows_of : (2 * chunk + 2) * rows_of]
                sums_ref[chunk, :, :out_dim] = jnp.where(core == 0, low, high)
                sums_ref[chunk, :, out_dim:] = side


def backward_kernel(
    place_ref, back_ref, source_ref, keep_ref, send_ref, total_ref, held_ref, arrived
):
    step = pl.program_id(0)
    values_ref = streamed(step, source_ref, held_ref, arrived)

    @pl.when(step == 0)
    def _():
        total_ref[...] = jnp.zeros_like(total_ref)

    for sub in range(STEP_TILES):
        rows = slice(sub * TILE, (sub + 1) * TILE)
        back = back_ref[:, rows]
        for pair in range(SLOTS // 2):
            term = jnp.dot(
                back,
                values_ref[:, 2 * pair * TILE : (2 * pair + 2) * TILE],
                preferred_element_type=jnp.float32,
            )
            for half in range(2):
                spot = place_ref[step * STEP_TILES + sub, 2 * pair + half]
                total_ref[spot] += term[:, half * TILE : (half + 1) * TILE]

    @pl.when(step == pl.num_programs(0) - 1)
    def _():
        half = DUMMY // 2
        keep_ref[...] = total_ref[:half].astype(jnp.bfloat16)
        send_ref[...] = total_ref[half : 2 * half].astype(jnp.bfloat16)


def layer(features, weight, bias, tile_values, tile_cols, tile_counts, out_grad):
    rows_dev, in_dim = features.shape
    out_dim = weight.shape[1]
    row_tiles = rows_dev // TILE
    nodes = rows_dev * lax.axis_size(AXES)
    factor = 1.0 / math.sqrt(nodes)
    rep = lax.axis_index(("y_hi", "core"))
    core = lax.axis_index("core")
    chunks = lax.axis_size(NEAR)
    chunk_rows = in_dim // (2 * chunks)
    step_rows = STEP_TILES * TILE

    other_row = to_row(features)
    pieces = {0: (features, other_row)}
    for steps in (1, -1):
        pieces[-steps] = (to_block(features, steps), to_block(other_row, steps))
    near = [piece for offset in (-1, 0, 1) for piece in pieces[offset]]
    far = [to_core(piece) for piece in near]
    blank = jnp.zeros_like(features)
    window = jnp.stack(near + far + [blank]).reshape(-1, TILE, in_dim)

    block_tile = tile_cols % (GROUP * PIECE_TILES)
    offset = tile_cols // (GROUP * PIECE_TILES)
    turn = (block_tile // PIECE_TILES) ^ rep
    place = ((turn & 1) * (PIECES // 2) + offset * 2 + (turn >> 1)) * PIECE_TILES
    place = place + block_tile % PIECE_TILES
    is_live = jnp.arange(SLOTS)[None, :] < tile_counts[:, None]
    place = jnp.where(is_live, place, DUMMY).astype(jnp.int32)

    tile_values = pltpu.with_memory_space_constraint(tile_values, pltpu.HBM)
    held = [
        pltpu.VMEM((row_tiles, TILE, SLOTS * TILE), jnp.bfloat16),
        pltpu.SemaphoreType.DMA((row_tiles,)),
    ]
    whole = lambda *shape: pl.BlockSpec(shape, lambda i, *_: (0,) * len(shape))
    act, back, own_sums, other_sums = pl.pallas_call(
        functools.partial(forward_kernel, factor),
        out_shape=(
            jax.ShapeDtypeStruct((rows_dev, out_dim), jnp.bfloat16),
            jax.ShapeDtypeStruct((in_dim, rows_dev), jnp.bfloat16),
            jax.ShapeDtypeStruct((chunks, chunk_rows, out_dim + TILE), jnp.float32),
            jax.ShapeDtypeStruct((chunks, chunk_rows, out_dim + TILE), jnp.float32),
        ),
        grid_spec=pltpu.PrefetchScalarGridSpec(
            num_scalar_prefetch=2,
            grid=(row_tiles // STEP_TILES,),
            in_specs=[
                whole(*window.shape),
                pl.BlockSpec(memory_space=pltpu.HBM),
                pl.BlockSpec((step_rows, out_dim), lambda i, *_: (i, 0)),
                whole(in_dim, out_dim),
                whole(1, out_dim),
            ],
            out_specs=(
                pl.BlockSpec((step_rows, out_dim), lambda i, *_: (i, 0)),
                pl.BlockSpec((in_dim, step_rows), lambda i, *_: (0, i)),
                whole(chunks, chunk_rows, out_dim + TILE),
                whole(chunks, chunk_rows, out_dim + TILE),
            ),
            scratch_shapes=[
                pltpu.VMEM((rows_dev, in_dim), jnp.bfloat16),
                pltpu.VMEM((rows_dev, out_dim), jnp.bfloat16),
                pltpu.VMEM((row_tiles * 8, out_dim), jnp.float32),
                *held,
            ],
        ),
        compiler_params=pltpu.CompilerParams(vmem_limit_bytes=VMEM_LIMIT),
        cost_estimate=pl.CostEstimate(flops=3 << 30, bytes_accessed=15 << 20, transcendentals=1 << 19),
        name="forward",
    )(place, core.reshape(1).astype(jnp.int32), window, tile_values, out_grad, weight, bias.reshape(1, -1))

    half_tiles = DUMMY // 2
    backward = pl.pallas_call(
        backward_kernel,
        out_shape=(jax.ShapeDtypeStruct((half_tiles, in_dim, TILE), jnp.bfloat16),) * 2,
        grid_spec=pltpu.PrefetchScalarGridSpec(
            num_scalar_prefetch=1,
            grid=(row_tiles // STEP_TILES,),
            in_specs=[
                pl.BlockSpec((in_dim, step_rows), lambda i, *_: (0, i)),
                pl.BlockSpec(memory_space=pltpu.HBM),
            ],
            out_specs=(whole(half_tiles, in_dim, TILE),) * 2,
            scratch_shapes=[pltpu.VMEM((DUMMY + 1, in_dim, TILE), jnp.float32), *held],
        ),
        compiler_params=pltpu.CompilerParams(vmem_limit_bytes=VMEM_LIMIT),
        cost_estimate=pl.CostEstimate(flops=2 << 30, bytes_accessed=12 << 20, transcendentals=0),
        name="backward",
    )
    keep, send = backward(place, back, tile_values)

    wide = lambda value: value.astype(jnp.float32)
    moved_sums = to_core(other_sums)
    part = own_sums + moved_sums
    from_core = to_core(send)
    part = jnp.sum(lax.all_to_all(part, NEAR, 0, 0, tiled=True), axis=0)
    part, from_core = lax.optimization_barrier((part, from_core))
    keep, from_core = (value.reshape(3, 2, -1, in_dim, TILE) for value in (keep, from_core))
    moved = []
    for steps in (1, -1):
        term = wide(keep[1 + steps]) + wide(from_core[1 + steps])
        moved.append(to_block(term.astype(jnp.bfloat16), steps))
    part = jnp.sum(to_all(part, FAR), axis=0)
    bias_grad = part[: out_dim // TILE, out_dim:].reshape(out_dim)
    total = wide(keep[1]) + wide(from_core[1]) + wide(moved[0]) + wide(moved[1])
    part, total = lax.optimization_barrier((part, jnp.swapaxes(total, 2, 3)))
    last = to_row(total[1].astype(jnp.bfloat16))
    mine = to_all(part[:, :out_dim], NEAR)
    theirs = to_core(mine)
    odd = core == 1
    weight_grad = jnp.stack([jnp.where(odd, theirs, mine), jnp.where(odd, mine, theirs)], axis=1)
    weight_grad = weight_grad.reshape(in_dim, out_dim)
    feature_grad = (total[0] + wide(last)).reshape(rows_dev, in_dim)
    return (act, feature_grad, weight_grad, bias_grad)


def solution(mesh):
    mesh = jax.sharding.Mesh(mesh.devices.reshape(SPLIT), AXES)
    in_specs = (
        P(AXES, None),
        P(),
        P(),
        P(AXES, None),
        P(AXES, None),
        P(AXES),
        P(AXES, None),
    )
    out_specs = (P(AXES, None), P(AXES, None), P(), P())
    return jax.shard_map(layer, mesh=mesh, in_specs=in_specs, out_specs=out_specs, check_vma=False)
```

```python
import functools
import math

import jax
import jax.numpy as jnp
from jax import lax
from jax.experimental import pallas as pl
from jax.experimental.pallas import tpu as pltpu
from jax.sharding import PartitionSpec as P


TILE = 128
REACH = 1
SLOTS = 32
GROUP = 4
PIECE_TILES = 8
PIECES = (2 * REACH + 1) * GROUP
DUMMY = PIECES * PIECE_TILES
AXES = ("y_lo", "z", "x", "y_hi", "core")
NEAR = ("x", "y_hi")
FAR = ("y_lo", "z")
VMEM_LIMIT = 32 << 20
SPLIT = (2, 8, 4, 2, 2)
STEP_TILES = 1


def sent(value, target):
    count = lax.axis_size(AXES)
    return lax.ppermute(value, AXES, [(source, target(source, count)) for source in range(count)])


def to_core(value):
    return sent(value, lambda device, count: device ^ 1)


def to_row(value):
    return sent(value, lambda device, count: device ^ 2)


def to_block(value, steps):
    return sent(value, lambda device, count: (device + GROUP * steps) % count)


def to_all(value, axes):
    count = lax.axis_size(axes)
    copies = jnp.broadcast_to(value[None], (count,) + value.shape)
    return lax.all_to_all(copies, axes, 0, 0, tiled=True)


def gelu_parts(pre_act):
    inner = 0.7978845608028654 * (pre_act + 0.044715 * pre_act * pre_act * pre_act)
    tangent = jnp.tanh(inner)
    value_part = 0.5 * pre_act * (1.0 + tangent)
    slope = 0.5 * (1.0 + tangent) + 0.5 * pre_act * (
        1.0 - tangent * tangent
    ) * 0.7978845608028654 * (1.0 + 0.134145 * pre_act * pre_act)
    return (value_part, slope)


def load_kernel(source_ref, held_ref, arrived):
    count = arrived.shape[0]
    rows = source_ref.shape[0] // count
    copies = [
        pltpu.make_async_copy(
            source_ref.at[pl.ds(i * rows, rows)], held_ref.at[pl.ds(i * rows, rows)], arrived.at[i]
        )
        for i in range(count)
    ]
    for copy in copies:
        copy.start()
    for copy in copies:
        copy.wait()


def merge_kernel(keep_ref, core_ref, up_ref, down_ref, own_ref, other_ref):
    for row in range(2):
        for tile in range(PIECE_TILES):
            refs = (keep_ref.at[1], core_ref.at[1], up_ref, down_ref)
            terms = [ref[row, tile].astype(jnp.float32) for ref in refs]
            total = jnp.swapaxes(terms[0] + terms[1] + terms[2] + terms[3], 0, 1)
            rows = slice(tile * TILE, (tile + 1) * TILE)
            if row == 0:
                own_ref[rows, :] = total
            else:
                other_ref[rows, :] = total.astype(jnp.bfloat16)


def forward_kernel(
    factor, place_ref, core_ref, window_ref, values_ref, grad_ref, weight_ref, bias_ref,
    act_ref, back_ref, own_ref, other_ref, agg_ref, pre_ref, bias_sum_ref,
):
    step = pl.program_id(0)
    weight = weight_ref[...]
    for sub in range(STEP_TILES):
        rows = slice(sub * TILE, (sub + 1) * TILE)
        tile = step * STEP_TILES + sub
        place = pl.ds(pl.multiple_of(tile * TILE, TILE), TILE)
        total = None
        for pair in range(SLOTS // 2):
            one = window_ref[place_ref[tile, 2 * pair]]
            two = window_ref[place_ref[tile, 2 * pair + 1]]
            term = jnp.dot(
                values_ref[place, 2 * pair * TILE : (2 * pair + 2) * TILE],
                jnp.concatenate([one, two], axis=0),
                preferred_element_type=jnp.float32,
            )
            total = term if total is None else total + term
        aggregated = total.astype(jnp.bfloat16)
        pre_act = jnp.dot(aggregated, weight, preferred_element_type=jnp.float32) + bias_ref[...]
        value_part, slope = gelu_parts(pre_act)
        act_ref[rows, :] = value_part.astype(jnp.bfloat16)
        pre_wide = (grad_ref[rows, :].astype(jnp.float32) * slope).astype(jnp.bfloat16)
        back_ref[:, rows] = lax.dot_general(
            weight, pre_wide, (((1,), (1,)), ((), ())), preferred_element_type=jnp.float32
        ).astype(jnp.bfloat16)
        agg_ref[place, :] = aggregated
        pre_ref[place, :] = pre_wide
        part = jnp.sum(pre_wide.astype(jnp.float32).reshape(TILE // 8, 8, -1), axis=0)
        bias_sum_ref[pl.ds(pl.multiple_of(tile * 8, 8), 8), :] = part

    @pl.when(step == pl.num_programs(0) - 1)
    def _():
        sums = factor * lax.dot_general(
            agg_ref[...], pre_ref[...], (((0,), (0,)), ((), ())), preferred_element_type=jnp.float32
        )
        bias_sum = jnp.sum(bias_sum_ref[...], axis=0, keepdims=True) * factor
        count, rows_of, _ = own_ref.shape
        out_dim = sums.shape[1]
        parts = [bias_sum[:, i * TILE : (i + 1) * TILE] for i in range(out_dim // TILE)]
        parts.append(jnp.zeros((rows_of - len(parts), TILE), jnp.float32))
        side = jnp.concatenate(parts, axis=0)
        for turn, sums_ref in enumerate((own_ref, other_ref)):
            core = jnp.bitwise_xor(core_ref[0], turn)
            for chunk in range(count):
                low = sums[2 * chunk * rows_of : (2 * chunk + 1) * rows_of]
                high = sums[(2 * chunk + 1) * rows_of : (2 * chunk + 2) * rows_of]
                sums_ref[chunk, :, :out_dim] = jnp.where(core == 0, low, high)
                sums_ref[chunk, :, out_dim:] = side


def backward_kernel(
    place_ref, back_ref, values_ref, keep_ref, send_ref, total_ref
):
    step = pl.program_id(0)

    @pl.when(step == 0)
    def _():
        total_ref[...] = jnp.zeros_like(total_ref)

    for sub in range(STEP_TILES):
        rows = slice(sub * TILE, (sub + 1) * TILE)
        back = back_ref[:, rows]
        tile = step * STEP_TILES + sub
        place = pl.ds(pl.multiple_of(tile * TILE, TILE), TILE)
        for pair in range(SLOTS // 2):
            term = jnp.dot(
                back,
                values_ref[place, 2 * pair * TILE : (2 * pair + 2) * TILE],
                preferred_element_type=jnp.float32,
            )
            for half in range(2):
                spot = place_ref[step * STEP_TILES + sub, 2 * pair + half]
                total_ref[spot] += term[:, half * TILE : (half + 1) * TILE]

    @pl.when(step == pl.num_programs(0) - 1)
    def _():
        half = DUMMY // 2
        keep_ref[...] = total_ref[:half].astype(jnp.bfloat16)
        send_ref[...] = total_ref[half : 2 * half].astype(jnp.bfloat16)


def layer(features, weight, bias, tile_values, tile_cols, tile_counts, out_grad):
    rows_dev, in_dim = features.shape
    out_dim = weight.shape[1]
    row_tiles = rows_dev // TILE
    nodes = rows_dev * lax.axis_size(AXES)
    factor = 1.0 / math.sqrt(nodes)
    rep = lax.axis_index(("y_hi", "core"))
    core = lax.axis_index("core")
    chunks = lax.axis_size(NEAR)
    chunk_rows = in_dim // (2 * chunks)
    step_rows = STEP_TILES * TILE

    other_row = to_row(features)
    pieces = {0: (features, other_row)}
    for steps in (1, -1):
        near = to_block(features, steps)
        far = to_block(other_row, steps)
        pieces[-steps] = (near, far)
    near = [piece for offset in (-1, 0, 1) for piece in pieces[offset]]
    far = [to_core(piece) for piece in near]
    blank = jnp.zeros_like(features)
    window = jnp.stack(near + far + [blank]).reshape(-1, TILE, in_dim)

    block_tile = tile_cols % (GROUP * PIECE_TILES)
    offset = tile_cols // (GROUP * PIECE_TILES)
    turn = (block_tile // PIECE_TILES) ^ rep
    place = ((turn & 1) * (PIECES // 2) + offset * 2 + (turn >> 1)) * PIECE_TILES
    place = place + block_tile % PIECE_TILES
    is_live = jnp.arange(SLOTS)[None, :] < tile_counts[:, None]
    place = jnp.where(is_live, place, DUMMY).astype(jnp.int32)

    load = pl.pallas_call(
        load_kernel,
        out_shape=pltpu.VMEM(tile_values.shape, tile_values.dtype),
        in_specs=[pl.BlockSpec(memory_space=pltpu.HBM)],
        out_specs=pl.BlockSpec(memory_space=pltpu.VMEM),
        scratch_shapes=[pltpu.SemaphoreType.DMA((row_tiles,))],
        compiler_params=pltpu.CompilerParams(vmem_limit_bytes=1 << 20),
        cost_estimate=pl.CostEstimate(flops=0, bytes_accessed=16 << 20, transcendentals=0),
        name="load",
    )
    tile_values = load(tile_values)
    whole = lambda *shape: pl.BlockSpec(shape, lambda i, *_: (0,) * len(shape))
    act, back, own_sums, other_sums = pl.pallas_call(
        functools.partial(forward_kernel, factor),
        out_shape=(
            jax.ShapeDtypeStruct((rows_dev, out_dim), jnp.bfloat16),
            jax.ShapeDtypeStruct((in_dim, rows_dev), jnp.bfloat16),
            jax.ShapeDtypeStruct((chunks, chunk_rows, out_dim + TILE), jnp.float32),
            jax.ShapeDtypeStruct((chunks, chunk_rows, out_dim + TILE), jnp.float32),
        ),
        grid_spec=pltpu.PrefetchScalarGridSpec(
            num_scalar_prefetch=2,
            grid=(row_tiles // STEP_TILES,),
            in_specs=[
                whole(*window.shape),
                pl.BlockSpec(memory_space=pltpu.VMEM),
                pl.BlockSpec((step_rows, out_dim), lambda i, *_: (i, 0)),
                whole(in_dim, out_dim),
                whole(1, out_dim),
            ],
            out_specs=(
                pl.BlockSpec((step_rows, out_dim), lambda i, *_: (i, 0)),
                pl.BlockSpec((in_dim, step_rows), lambda i, *_: (0, i)),
                whole(chunks, chunk_rows, out_dim + TILE),
                whole(chunks, chunk_rows, out_dim + TILE),
            ),
            scratch_shapes=[
                pltpu.VMEM((rows_dev, in_dim), jnp.bfloat16),
                pltpu.VMEM((rows_dev, out_dim), jnp.bfloat16),
                pltpu.VMEM((row_tiles * 8, out_dim), jnp.float32),
            ],
        ),
        compiler_params=pltpu.CompilerParams(vmem_limit_bytes=VMEM_LIMIT),
        cost_estimate=pl.CostEstimate(flops=3 << 30, bytes_accessed=15 << 20, transcendentals=1 << 19),
        name="forward",
    )(place, core.reshape(1).astype(jnp.int32), window, tile_values, out_grad, weight, bias.reshape(1, -1))

    half_tiles = DUMMY // 2
    backward = pl.pallas_call(
        backward_kernel,
        out_shape=(jax.ShapeDtypeStruct((half_tiles, in_dim, TILE), jnp.bfloat16),) * 2,
        grid_spec=pltpu.PrefetchScalarGridSpec(
            num_scalar_prefetch=1,
            grid=(row_tiles // STEP_TILES,),
            in_specs=[
                pl.BlockSpec((in_dim, step_rows), lambda i, *_: (0, i)),
                pl.BlockSpec(memory_space=pltpu.VMEM),
            ],
            out_specs=(whole(half_tiles, in_dim, TILE),) * 2,
            scratch_shapes=[pltpu.VMEM((DUMMY + 1, in_dim, TILE), jnp.float32)],
        ),
        compiler_params=pltpu.CompilerParams(vmem_limit_bytes=VMEM_LIMIT),
        cost_estimate=pl.CostEstimate(flops=2 << 30, bytes_accessed=12 << 20, transcendentals=0),
        name="backward",
    )
    keep, send = backward(place, back, tile_values)

    wide = lambda value: value.astype(jnp.float32)
    moved_sums = to_core(other_sums)
    part = own_sums + moved_sums
    from_core = to_core(send)
    part = jnp.sum(lax.all_to_all(part, NEAR, 0, 0, tiled=True), axis=0)
    part, from_core = lax.optimization_barrier((part, from_core))
    keep, from_core = (value.reshape(3, 2, -1, in_dim, TILE) for value in (keep, from_core))
    moved = []
    for steps in (1, -1):
        term = wide(keep[1 + steps]) + wide(from_core[1 + steps])
        moved.append(to_block(term.astype(jnp.bfloat16), steps))
    part = jnp.sum(to_all(part, FAR), axis=0)
    bias_grad = part[: out_dim // TILE, out_dim:].reshape(out_dim)
    own, other = pl.pallas_call(
        merge_kernel,
        out_shape=(
            jax.ShapeDtypeStruct((rows_dev, in_dim), jnp.float32),
            jax.ShapeDtypeStruct((rows_dev, in_dim), jnp.bfloat16),
        ),
        compiler_params=pltpu.CompilerParams(vmem_limit_bytes=16 << 20),
        cost_estimate=pl.CostEstimate(flops=1 << 20, bytes_accessed=4 << 20, transcendentals=0),
        name="merge",
    )(keep, from_core, moved[0], moved[1])
    last = to_row(other)
    mine = to_all(part[:, :out_dim], NEAR)
    theirs = to_core(mine)
    odd = core == 1
    weight_grad = jnp.stack([jnp.where(odd, theirs, mine), jnp.where(odd, mine, theirs)], axis=1)
    weight_grad = weight_grad.reshape(in_dim, out_dim)
    feature_grad = own + wide(last)
    return (act, feature_grad, weight_grad, bias_grad)


def solution(mesh):
    mesh = jax.sharding.Mesh(mesh.devices.reshape(SPLIT), AXES)
    in_specs = (
        P(AXES, None),
        P(),
        P(),
        P(AXES, None),
        P(AXES, None),
        P(AXES),
        P(AXES, None),
    )
    out_specs = (P(AXES, None), P(AXES, None), P(), P())
    return jax.shard_map(layer, mesh=mesh, in_specs=in_specs, out_specs=out_specs, check_vma=False)
```

```python
import functools
import math

import jax
import jax.numpy as jnp
from jax import lax
from jax.experimental import pallas as pl
from jax.experimental.pallas import tpu as pltpu
from jax.sharding import PartitionSpec as P


TILE = 128
REACH = 1
SLOTS = 32
GROUP = 4
PIECE_TILES = 8
PIECES = (2 * REACH + 1) * GROUP
DUMMY = PIECES * PIECE_TILES
AXES = ("y_lo", "z", "x", "y_hi", "core")
NEAR = ("x", "y_hi")
FAR = ("y_lo", "z")
VMEM_LIMIT = 14 << 20
SPLIT = (2, 8, 4, 2, 2)
STEP_TILES = 1


def sent(value, target):
    count = lax.axis_size(AXES)
    return lax.ppermute(value, AXES, [(source, target(source, count)) for source in range(count)])


def to_core(value):
    return sent(value, lambda device, count: device ^ 1)


def to_row(value):
    return sent(value, lambda device, count: device ^ 2)


def to_block(value, steps):
    return sent(value, lambda device, count: (device + GROUP * steps) % count)


def to_all(value, axes):
    count = lax.axis_size(axes)
    copies = jnp.broadcast_to(value[None], (count,) + value.shape)
    return lax.all_to_all(copies, axes, 0, 0, tiled=True)


def gelu_parts(pre_act):
    inner = 0.7978845608028654 * (pre_act + 0.044715 * pre_act * pre_act * pre_act)
    tangent = jnp.tanh(inner)
    value_part = 0.5 * pre_act * (1.0 + tangent)
    slope = 0.5 * (1.0 + tangent) + 0.5 * pre_act * (
        1.0 - tangent * tangent
    ) * 0.7978845608028654 * (1.0 + 0.134145 * pre_act * pre_act)
    return (value_part, slope)


def load_kernel(source_ref, held_ref, arrived):
    count = arrived.shape[0]
    rows = source_ref.shape[0] // count
    copies = [
        pltpu.make_async_copy(
            source_ref.at[pl.ds(i * rows, rows)], held_ref.at[pl.ds(i * rows, rows)], arrived.at[i]
        )
        for i in range(count)
    ]
    for copy in copies:
        copy.start()
    for copy in copies:
        copy.wait()


def turned(refs, index):
    terms = [ref[index].astype(jnp.float32) for ref in refs]
    return jnp.swapaxes(terms[0] + terms[1] + terms[2] + terms[3], 0, 1)


def merge_kernel(keep_ref, core_ref, up_ref, down_ref, out_ref):
    refs = (keep_ref.at[0, 0], core_ref.at[0, 0], up_ref.at[0], down_ref.at[0])
    for tile in range(PIECE_TILES):
        out_ref[tile * TILE : (tile + 1) * TILE, :] = turned(refs, tile).astype(jnp.bfloat16)


def final_kernel(keep_ref, core_ref, up_ref, down_ref, last_ref, out_ref):
    refs = (keep_ref.at[0, 0], core_ref.at[0, 0], up_ref.at[0], down_ref.at[0])
    for tile in range(out_ref.shape[0] // TILE):
        rows = slice(tile * TILE, (tile + 1) * TILE)
        out_ref[rows, :] = turned(refs, tile) + last_ref[rows, :].astype(jnp.float32)


def forward_kernel(
    factor, place_ref, core_ref, window_ref, values_ref, grad_ref, weight_ref, bias_ref,
    act_ref, back_ref, own_ref, other_ref, agg_ref, pre_ref, bias_sum_ref,
):
    step = pl.program_id(0)
    weight = weight_ref[...]
    for sub in range(STEP_TILES):
        rows = slice(sub * TILE, (sub + 1) * TILE)
        tile = step * STEP_TILES + sub
        place = pl.ds(pl.multiple_of(tile * TILE, TILE), TILE)
        total = None
        for pair in range(SLOTS // 2):
            one = window_ref[place_ref[tile, 2 * pair]]
            two = window_ref[place_ref[tile, 2 * pair + 1]]
            term = jnp.dot(
                values_ref[place, 2 * pair * TILE : (2 * pair + 2) * TILE],
                jnp.concatenate([one, two], axis=0),
                preferred_element_type=jnp.float32,
            )
            total = term if total is None else total + term
        aggregated = total.astype(jnp.bfloat16)
        pre_act = jnp.dot(aggregated, weight, preferred_element_type=jnp.float32) + bias_ref[...]
        value_part, slope = gelu_parts(pre_act)
        act_ref[rows, :] = value_part.astype(jnp.bfloat16)
        pre_wide = (grad_ref[rows, :].astype(jnp.float32) * slope).astype(jnp.bfloat16)
        back_ref[tile] = lax.dot_general(
            weight, pre_wide, (((1,), (1,)), ((), ())), preferred_element_type=jnp.float32
        ).astype(jnp.bfloat16)
        agg_ref[place, :] = aggregated
        pre_ref[place, :] = pre_wide
        part = jnp.sum(pre_wide.astype(jnp.float32).reshape(TILE // 8, 8, -1), axis=0)
        bias_sum_ref[pl.ds(pl.multiple_of(tile * 8, 8), 8), :] = part

    @pl.when(step == pl.num_programs(0) - 1)
    def _():
        sums = factor * lax.dot_general(
            agg_ref[...], pre_ref[...], (((0,), (0,)), ((), ())), preferred_element_type=jnp.float32
        )
        bias_sum = jnp.sum(bias_sum_ref[...], axis=0, keepdims=True) * factor
        count, rows_of, _ = own_ref.shape
        out_dim = sums.shape[1]
        parts = [bias_sum[:, i * TILE : (i + 1) * TILE] for i in range(out_dim // TILE)]
        parts.append(jnp.zeros((rows_of - len(parts), TILE), jnp.float32))
        side = jnp.concatenate(parts, axis=0)
        for turn, sums_ref in enumerate((own_ref, other_ref)):
            core = jnp.bitwise_xor(core_ref[0], turn)
            for chunk in range(count):
                low = sums[2 * chunk * rows_of : (2 * chunk + 1) * rows_of]
                high = sums[(2 * chunk + 1) * rows_of : (2 * chunk + 2) * rows_of]
                sums_ref[chunk, :, :out_dim] = jnp.where(core == 0, low, high)
                sums_ref[chunk, :, out_dim:] = side


def backward_kernel(
    place_ref, back_ref, values_ref, keep_ref, send_ref, total_ref
):
    step = pl.program_id(0)

    @pl.when(step == 0)
    def _():
        total_ref[...] = jnp.zeros_like(total_ref)

    for sub in range(STEP_TILES):
        tile = step * STEP_TILES + sub
        back = back_ref[tile]
        place = pl.ds(pl.multiple_of(tile * TILE, TILE), TILE)
        for pair in range(SLOTS // 2):
            term = jnp.dot(
                back,
                values_ref[place, 2 * pair * TILE : (2 * pair + 2) * TILE],
                preferred_element_type=jnp.float32,
            )
            for half in range(2):
                spot = place_ref[step * STEP_TILES + sub, 2 * pair + half]
                total_ref[spot] += term[:, half * TILE : (half + 1) * TILE]

    @pl.when(step == pl.num_programs(0) - 1)
    def _():
        half = DUMMY // 2
        keep_ref[...] = total_ref[:half].astype(jnp.bfloat16)
        send_ref[...] = total_ref[half : 2 * half].astype(jnp.bfloat16)


def layer(features, weight, bias, tile_values, tile_cols, tile_counts, out_grad):
    rows_dev, in_dim = features.shape
    out_dim = weight.shape[1]
    row_tiles = rows_dev // TILE
    nodes = rows_dev * lax.axis_size(AXES)
    factor = 1.0 / math.sqrt(nodes)
    rep = lax.axis_index(("y_hi", "core"))
    core = lax.axis_index("core")
    chunks = lax.axis_size(NEAR)
    chunk_rows = in_dim // (2 * chunks)
    step_rows = STEP_TILES * TILE

    other_row = to_row(features)
    pieces = {0: (features, other_row)}
    for steps in (1, -1):
        near = to_block(features, steps)
        far = to_block(other_row, steps)
        pieces[-steps] = (near, far)
    near = [piece for offset in (-1, 0, 1) for piece in pieces[offset]]
    far = [to_core(piece) for piece in near]
    blank = jnp.zeros_like(features)
    window = jnp.stack(near + far + [blank]).reshape(-1, TILE, in_dim)

    block_tile = tile_cols % (GROUP * PIECE_TILES)
    offset = tile_cols // (GROUP * PIECE_TILES)
    turn = (block_tile // PIECE_TILES) ^ rep
    place = ((turn & 1) * (PIECES // 2) + offset * 2 + (turn >> 1)) * PIECE_TILES
    place = place + block_tile % PIECE_TILES
    is_live = jnp.arange(SLOTS)[None, :] < tile_counts[:, None]
    place = jnp.where(is_live, place, DUMMY).astype(jnp.int32)

    load = pl.pallas_call(
        load_kernel,
        out_shape=pltpu.VMEM(tile_values.shape, tile_values.dtype),
        in_specs=[pl.BlockSpec(memory_space=pltpu.HBM)],
        out_specs=pl.BlockSpec(memory_space=pltpu.VMEM),
        scratch_shapes=[pltpu.SemaphoreType.DMA((row_tiles,))],
        compiler_params=pltpu.CompilerParams(vmem_limit_bytes=1 << 20),
        cost_estimate=pl.CostEstimate(flops=0, bytes_accessed=16 << 20, transcendentals=0),
        name="load",
    )
    tile_values = load(pltpu.with_memory_space_constraint(tile_values, pltpu.HBM))
    whole = pl.BlockSpec(memory_space=pltpu.VMEM)
    act, back, own_sums, other_sums = pl.pallas_call(
        functools.partial(forward_kernel, factor),
        out_shape=(
            jax.ShapeDtypeStruct((rows_dev, out_dim), jnp.bfloat16),
            jax.ShapeDtypeStruct((row_tiles, in_dim, TILE), jnp.bfloat16),
            jax.ShapeDtypeStruct((chunks, chunk_rows, out_dim + TILE), jnp.float32),
            jax.ShapeDtypeStruct((chunks, chunk_rows, out_dim + TILE), jnp.float32),
        ),
        grid_spec=pltpu.PrefetchScalarGridSpec(
            num_scalar_prefetch=2,
            grid=(row_tiles // STEP_TILES,),
            in_specs=[
                whole,
                whole,
                pl.BlockSpec((step_rows, out_dim), lambda i, *_: (i, 0)),
                whole,
                whole,
            ],
            out_specs=(
                pl.BlockSpec((step_rows, out_dim), lambda i, *_: (i, 0)),
                whole,
                whole,
                whole,
            ),
            scratch_shapes=[
                pltpu.VMEM((rows_dev, in_dim), jnp.bfloat16),
                pltpu.VMEM((rows_dev, out_dim), jnp.bfloat16),
                pltpu.VMEM((row_tiles * 8, out_dim), jnp.float32),
            ],
        ),
        compiler_params=pltpu.CompilerParams(vmem_limit_bytes=VMEM_LIMIT),
        cost_estimate=pl.CostEstimate(flops=3 << 30, bytes_accessed=15 << 20, transcendentals=1 << 19),
        name="forward",
    )(place, core.reshape(1).astype(jnp.int32), window, tile_values, out_grad, weight, bias.reshape(1, -1))

    half_tiles = DUMMY // 2
    backward = pl.pallas_call(
        backward_kernel,
        out_shape=(jax.ShapeDtypeStruct((half_tiles, in_dim, TILE), jnp.bfloat16),) * 2,
        grid_spec=pltpu.PrefetchScalarGridSpec(
            num_scalar_prefetch=1,
            grid=(row_tiles // STEP_TILES,),
            in_specs=[
                whole,
                whole,
            ],
            out_specs=(whole,) * 2,
            scratch_shapes=[pltpu.VMEM((DUMMY + 1, in_dim, TILE), jnp.float32)],
        ),
        compiler_params=pltpu.CompilerParams(vmem_limit_bytes=VMEM_LIMIT),
        cost_estimate=pl.CostEstimate(flops=2 << 30, bytes_accessed=12 << 20, transcendentals=0),
        name="backward",
    )
    keep, send = backward(place, back, tile_values)

    wide = lambda value: value.astype(jnp.float32)
    moved_sums = to_core(other_sums)
    part = own_sums + moved_sums
    from_core = to_core(send)
    part = jnp.sum(lax.all_to_all(part, NEAR, 0, 0, tiled=True), axis=0)
    part, from_core = lax.optimization_barrier((part, from_core))
    keep, from_core = (value.reshape(3, 2, -1, in_dim, TILE) for value in (keep, from_core))
    moved = []
    for steps in (1, -1):
        term = wide(keep[1 + steps]) + wide(from_core[1 + steps])
        moved.append(to_block(term.astype(jnp.bfloat16), steps))
    part = to_all(part, FAR)
    part = jnp.sum(part, axis=0)
    bias_grad = part[: out_dim // TILE, out_dim:].reshape(out_dim)

    def pieces_of(row, tiles):
        outer = pl.BlockSpec((1, 1, tiles, in_dim, TILE), lambda i: (1, row, i, 0, 0))
        inner = pl.BlockSpec((1, tiles, in_dim, TILE), lambda i: (row, i, 0, 0))
        return [outer, outer, inner, inner]

    operands = (keep, from_core, moved[0], moved[1])
    other = pl.pallas_call(
        merge_kernel,
        out_shape=jax.ShapeDtypeStruct((rows_dev, in_dim), jnp.bfloat16),
        grid=(1,),
        in_specs=pieces_of(1, PIECE_TILES),
        out_specs=pl.BlockSpec((rows_dev, in_dim), lambda i: (0, 0)),
        compiler_params=pltpu.CompilerParams(vmem_limit_bytes=6 << 20),
        cost_estimate=pl.CostEstimate(flops=1 << 20, bytes_accessed=2 << 20, transcendentals=0),
        name="merge",
    )(*operands)
    last = to_row(other)
    mine = to_all(part[:, :out_dim], NEAR)
    theirs = to_core(mine)
    odd = core == 1
    weight_grad = jnp.stack([jnp.where(odd, theirs, mine), jnp.where(odd, mine, theirs)], axis=1)
    weight_grad = weight_grad.reshape(in_dim, out_dim)
    final_tiles = 2
    rows_spec = pl.BlockSpec((final_tiles * TILE, in_dim), lambda i: (i, 0))
    feature_grad = pl.pallas_call(
        final_kernel,
        out_shape=jax.ShapeDtypeStruct((rows_dev, in_dim), jnp.float32),
        grid=(PIECE_TILES // final_tiles,),
        in_specs=[*pieces_of(0, final_tiles), rows_spec],
        out_specs=rows_spec,
        compiler_params=pltpu.CompilerParams(vmem_limit_bytes=6 << 20),
        cost_estimate=pl.CostEstimate(flops=1 << 20, bytes_accessed=2 << 20, transcendentals=0),
        name="final",
    )(*operands, last)
    return (act, feature_grad, weight_grad, bias_grad)


def solution(mesh):
    mesh = jax.sharding.Mesh(mesh.devices.reshape(SPLIT), AXES)
    in_specs = (
        P(AXES, None),
        P(),
        P(),
        P(AXES, None),
        P(AXES, None),
        P(AXES),
        P(AXES, None),
    )
    out_specs = (P(AXES, None), P(AXES, None), P(), P())
    return jax.shard_map(layer, mesh=mesh, in_specs=in_specs, out_specs=out_specs, check_vma=False)
```

```python
import functools
import math

import jax
import jax.numpy as jnp
from jax import lax
from jax.experimental import pallas as pl
from jax.experimental.pallas import tpu as pltpu
from jax.sharding import PartitionSpec as P


TILE = 128
REACH = 1
SLOTS = 32
GROUP = 4
PIECE_TILES = 8
PIECES = (2 * REACH + 1) * GROUP
DUMMY = PIECES * PIECE_TILES
AXES = ("y_lo", "z", "x", "y_hi", "core")
NEAR = ("x", "y_hi")
FAR = ("y_lo", "z")
VMEM_LIMIT = 14 << 20
SPLIT = (2, 8, 4, 2, 2)
STEP_TILES = 1


def sent(value, target):
    count = lax.axis_size(AXES)
    return lax.ppermute(value, AXES, [(source, target(source, count)) for source in range(count)])


def to_core(value):
    return sent(value, lambda device, count: device ^ 1)


def to_row(value):
    return sent(value, lambda device, count: device ^ 2)


def to_block(value, steps):
    return sent(value, lambda device, count: (device + GROUP * steps) % count)


def to_all(value, axes):
    count = lax.axis_size(axes)
    copies = jnp.broadcast_to(value[None], (count,) + value.shape)
    return lax.all_to_all(copies, axes, 0, 0, tiled=True)


def gelu_parts(pre_act):
    inner = 0.7978845608028654 * (pre_act + 0.044715 * pre_act * pre_act * pre_act)
    tangent = jnp.tanh(inner)
    value_part = 0.5 * pre_act * (1.0 + tangent)
    slope = 0.5 * (1.0 + tangent) + 0.5 * pre_act * (
        1.0 - tangent * tangent
    ) * 0.7978845608028654 * (1.0 + 0.134145 * pre_act * pre_act)
    return (value_part, slope)


def load_kernel(source_ref, held_ref, arrived):
    count = arrived.shape[0]
    rows = source_ref.shape[0] // count
    copies = [
        pltpu.make_async_copy(
            source_ref.at[pl.ds(i * rows, rows)], held_ref.at[pl.ds(i * rows, rows)], arrived.at[i]
        )
        for i in range(count)
    ]
    for copy in copies:
        copy.start()
    for copy in copies:
        copy.wait()


def turned(refs, index):
    terms = [ref[index].astype(jnp.float32) for ref in refs]
    return jnp.swapaxes(terms[0] + terms[1] + terms[2] + terms[3], 0, 1)


def merge_kernel(keep_ref, core_ref, up_ref, down_ref, out_ref):
    refs = (keep_ref.at[1, 1], core_ref.at[1, 1], up_ref.at[1], down_ref.at[1])
    for tile in range(PIECE_TILES):
        out_ref[tile * TILE : (tile + 1) * TILE, :] = turned(refs, tile).astype(jnp.bfloat16)


def final_kernel(keep_ref, core_ref, up_ref, down_ref, last_ref, out_ref):
    refs = (keep_ref.at[1, 0], core_ref.at[1, 0], up_ref.at[0], down_ref.at[0])
    count = out_ref.shape[0] // TILE
    for sub in range(count):
        tile = pl.program_id(0) * count + sub
        rows = pl.ds(pl.multiple_of(tile * TILE, TILE), TILE)
        total = turned(refs, tile) + last_ref[rows, :].astype(jnp.float32)
        out_ref[sub * TILE : (sub + 1) * TILE, :] = total


def forward_kernel(
    factor, place_ref, core_ref, window_ref, values_ref, grad_ref, weight_ref, bias_ref,
    act_ref, back_ref, own_ref, other_ref, agg_ref, pre_ref, bias_sum_ref,
):
    step = pl.program_id(0)
    weight = weight_ref[...]
    for sub in range(STEP_TILES):
        rows = slice(sub * TILE, (sub + 1) * TILE)
        tile = step * STEP_TILES + sub
        place = pl.ds(pl.multiple_of(tile * TILE, TILE), TILE)
        total = None
        for pair in range(SLOTS // 2):
            one = window_ref[place_ref[tile, 2 * pair]]
            two = window_ref[place_ref[tile, 2 * pair + 1]]
            term = jnp.dot(
                values_ref[place, 2 * pair * TILE : (2 * pair + 2) * TILE],
                jnp.concatenate([one, two], axis=0),
                preferred_element_type=jnp.float32,
            )
            total = term if total is None else total + term
        aggregated = total.astype(jnp.bfloat16)
        pre_act = jnp.dot(aggregated, weight, preferred_element_type=jnp.float32) + bias_ref[...]
        value_part, slope = gelu_parts(pre_act)
        act_ref[rows, :] = value_part.astype(jnp.bfloat16)
        pre_wide = (grad_ref[rows, :].astype(jnp.float32) * slope).astype(jnp.bfloat16)
        back_ref[tile] = lax.dot_general(
            weight, pre_wide, (((1,), (1,)), ((), ())), preferred_element_type=jnp.float32
        ).astype(jnp.bfloat16)
        agg_ref[place, :] = aggregated
        pre_ref[place, :] = pre_wide
        part = jnp.sum(pre_wide.astype(jnp.float32).reshape(TILE // 8, 8, -1), axis=0)
        bias_sum_ref[pl.ds(pl.multiple_of(tile * 8, 8), 8), :] = part

    @pl.when(step == pl.num_programs(0) - 1)
    def _():
        sums = factor * lax.dot_general(
            agg_ref[...], pre_ref[...], (((0,), (0,)), ((), ())), preferred_element_type=jnp.float32
        )
        bias_sum = jnp.sum(bias_sum_ref[...], axis=0, keepdims=True) * factor
        count, rows_of, _ = own_ref.shape
        out_dim = sums.shape[1]
        parts = [bias_sum[:, i * TILE : (i + 1) * TILE] for i in range(out_dim // TILE)]
        parts.append(jnp.zeros((rows_of - len(parts), TILE), jnp.float32))
        side = jnp.concatenate(parts, axis=0)
        for turn, sums_ref in enumerate((own_ref, other_ref)):
            core = jnp.bitwise_xor(core_ref[0], turn)
            for chunk in range(count):
                low = sums[2 * chunk * rows_of : (2 * chunk + 1) * rows_of]
                high = sums[(2 * chunk + 1) * rows_of : (2 * chunk + 2) * rows_of]
                sums_ref[chunk, :, :out_dim] = jnp.where(core == 0, low, high)
                sums_ref[chunk, :, out_dim:] = side


def backward_kernel(
    place_ref, back_ref, values_ref, keep_ref, send_ref, total_ref
):
    step = pl.program_id(0)

    @pl.when(step == 0)
    def _():
        total_ref[...] = jnp.zeros_like(total_ref)

    for sub in range(STEP_TILES):
        tile = step * STEP_TILES + sub
        back = back_ref[tile]
        place = pl.ds(pl.multiple_of(tile * TILE, TILE), TILE)
        for pair in range(SLOTS // 2):
            term = jnp.dot(
                back,
                values_ref[place, 2 * pair * TILE : (2 * pair + 2) * TILE],
                preferred_element_type=jnp.float32,
            )
            for half in range(2):
                spot = place_ref[step * STEP_TILES + sub, 2 * pair + half]
                total_ref[spot] += term[:, half * TILE : (half + 1) * TILE]

    @pl.when(step == pl.num_programs(0) - 1)
    def _():
        half = DUMMY // 2
        keep_ref[...] = total_ref[:half].astype(jnp.bfloat16)
        send_ref[...] = total_ref[half : 2 * half].astype(jnp.bfloat16)


def layer(features, weight, bias, tile_values, tile_cols, tile_counts, out_grad):
    rows_dev, in_dim = features.shape
    out_dim = weight.shape[1]
    row_tiles = rows_dev // TILE
    nodes = rows_dev * lax.axis_size(AXES)
    factor = 1.0 / math.sqrt(nodes)
    rep = lax.axis_index(("y_hi", "core"))
    core = lax.axis_index("core")
    chunks = lax.axis_size(NEAR)
    chunk_rows = in_dim // (2 * chunks)
    step_rows = STEP_TILES * TILE

    other_row = to_row(features)
    pieces = {0: (features, other_row)}
    for steps in (1, -1):
        near = to_block(features, steps)
        far = to_block(other_row, steps)
        pieces[-steps] = (near, far)
    near = [piece for offset in (-1, 0, 1) for piece in pieces[offset]]
    far = [to_core(piece) for piece in near]
    blank = jnp.zeros_like(features)
    window = jnp.stack(near + far + [blank]).reshape(-1, TILE, in_dim)

    block_tile = tile_cols % (GROUP * PIECE_TILES)
    offset = tile_cols // (GROUP * PIECE_TILES)
    turn = (block_tile // PIECE_TILES) ^ rep
    place = ((turn & 1) * (PIECES // 2) + offset * 2 + (turn >> 1)) * PIECE_TILES
    place = place + block_tile % PIECE_TILES
    is_live = jnp.arange(SLOTS)[None, :] < tile_counts[:, None]
    place = jnp.where(is_live, place, DUMMY).astype(jnp.int32)

    load = pl.pallas_call(
        load_kernel,
        out_shape=pltpu.VMEM(tile_values.shape, tile_values.dtype),
        in_specs=[pl.BlockSpec(memory_space=pltpu.HBM)],
        out_specs=pl.BlockSpec(memory_space=pltpu.VMEM),
        scratch_shapes=[pltpu.SemaphoreType.DMA((row_tiles,))],
        compiler_params=pltpu.CompilerParams(vmem_limit_bytes=1 << 20),
        cost_estimate=pl.CostEstimate(flops=0, bytes_accessed=16 << 20, transcendentals=0),
        name="load",
    )
    tile_values = load(pltpu.with_memory_space_constraint(tile_values, pltpu.HBM))
    whole = pl.BlockSpec(memory_space=pltpu.VMEM)
    act, back, own_sums, other_sums = pl.pallas_call(
        functools.partial(forward_kernel, factor),
        out_shape=(
            jax.ShapeDtypeStruct((rows_dev, out_dim), jnp.bfloat16),
            jax.ShapeDtypeStruct((row_tiles, in_dim, TILE), jnp.bfloat16),
            jax.ShapeDtypeStruct((chunks, chunk_rows, out_dim + TILE), jnp.float32),
            jax.ShapeDtypeStruct((chunks, chunk_rows, out_dim + TILE), jnp.float32),
        ),
        grid_spec=pltpu.PrefetchScalarGridSpec(
            num_scalar_prefetch=2,
            grid=(row_tiles // STEP_TILES,),
            in_specs=[
                whole,
                whole,
                pl.BlockSpec((step_rows, out_dim), lambda i, *_: (i, 0)),
                whole,
                whole,
            ],
            out_specs=(
                pl.BlockSpec((step_rows, out_dim), lambda i, *_: (i, 0)),
                whole,
                whole,
                whole,
            ),
            scratch_shapes=[
                pltpu.VMEM((rows_dev, in_dim), jnp.bfloat16),
                pltpu.VMEM((rows_dev, out_dim), jnp.bfloat16),
                pltpu.VMEM((row_tiles * 8, out_dim), jnp.float32),
            ],
        ),
        compiler_params=pltpu.CompilerParams(vmem_limit_bytes=VMEM_LIMIT),
        cost_estimate=pl.CostEstimate(flops=3 << 30, bytes_accessed=15 << 20, transcendentals=1 << 19),
        name="forward",
    )(place, core.reshape(1).astype(jnp.int32), window, tile_values, out_grad, weight, bias.reshape(1, -1))

    half_tiles = DUMMY // 2
    backward = pl.pallas_call(
        backward_kernel,
        out_shape=(jax.ShapeDtypeStruct((half_tiles, in_dim, TILE), jnp.bfloat16),) * 2,
        grid_spec=pltpu.PrefetchScalarGridSpec(
            num_scalar_prefetch=1,
            grid=(row_tiles // STEP_TILES,),
            in_specs=[
                whole,
                whole,
            ],
            out_specs=(whole,) * 2,
            scratch_shapes=[pltpu.VMEM((DUMMY + 1, in_dim, TILE), jnp.float32)],
        ),
        compiler_params=pltpu.CompilerParams(vmem_limit_bytes=VMEM_LIMIT),
        cost_estimate=pl.CostEstimate(flops=2 << 30, bytes_accessed=12 << 20, transcendentals=0),
        name="backward",
    )
    keep, send = backward(place, back, tile_values)

    wide = lambda value: value.astype(jnp.float32)
    moved_sums = to_core(other_sums)
    part = own_sums + moved_sums
    from_core = to_core(send)
    part = jnp.sum(lax.all_to_all(part, NEAR, 0, 0, tiled=True), axis=0)
    part, from_core = lax.optimization_barrier((part, from_core))
    keep, from_core = (value.reshape(3, 2, -1, in_dim, TILE) for value in (keep, from_core))
    moved = []
    for steps in (1, -1):
        term = wide(keep[1 + steps]) + wide(from_core[1 + steps])
        moved.append(to_block(term.astype(jnp.bfloat16), steps))
    part = to_all(part, FAR)
    part = jnp.sum(part, axis=0)
    bias_grad = part[: out_dim // TILE, out_dim:].reshape(out_dim)
    operands = (keep, from_core, moved[0], moved[1])
    other = pl.pallas_call(
        merge_kernel,
        out_shape=jax.ShapeDtypeStruct((rows_dev, in_dim), jnp.bfloat16),
        in_specs=[whole] * 4,
        out_specs=whole,
        compiler_params=pltpu.CompilerParams(vmem_limit_bytes=6 << 20),
        cost_estimate=pl.CostEstimate(flops=1 << 20, bytes_accessed=2 << 20, transcendentals=0),
        name="merge",
    )(*operands)
    last = to_row(other)
    mine = to_all(part[:, :out_dim], NEAR)
    theirs = to_core(mine)
    odd = core == 1
    weight_grad = jnp.stack([jnp.where(odd, theirs, mine), jnp.where(odd, mine, theirs)], axis=1)
    weight_grad = weight_grad.reshape(in_dim, out_dim)
    final_tiles = 2
    rows_spec = pl.BlockSpec((final_tiles * TILE, in_dim), lambda i: (i, 0))
    final = pl.pallas_call(
        final_kernel,
        out_shape=jax.ShapeDtypeStruct((rows_dev, in_dim), jnp.float32),
        grid=(PIECE_TILES // final_tiles,),
        in_specs=[whole] * 5,
        out_specs=rows_spec,
        compiler_params=pltpu.CompilerParams(vmem_limit_bytes=6 << 20),
        cost_estimate=pl.CostEstimate(flops=1 << 20, bytes_accessed=2 << 20, transcendentals=0),
        name="final",
    )
    feature_grad = final(*operands, last)
    return (act, feature_grad, weight_grad, bias_grad)


def solution(mesh):
    mesh = jax.sharding.Mesh(mesh.devices.reshape(SPLIT), AXES)
    in_specs = (
        P(AXES, None),
        P(),
        P(),
        P(AXES, None),
        P(AXES, None),
        P(AXES),
        P(AXES, None),
    )
    out_specs = (P(AXES, None), P(AXES, None), P(), P())
    return jax.shard_map(layer, mesh=mesh, in_specs=in_specs, out_specs=out_specs, check_vma=False)
```

```python
import functools
import math

import jax
import jax.numpy as jnp
from jax import lax
from jax.experimental import pallas as pl
from jax.experimental.pallas import tpu as pltpu
from jax.sharding import PartitionSpec as P


TILE = 128
REACH = 1
SLOTS = 32
GROUP = 4
PIECE_TILES = 8
PIECES = (2 * REACH + 1) * GROUP
DUMMY = PIECES * PIECE_TILES
AXES = ("y_lo", "z", "x", "y_hi", "core")
NEAR = ("x", "y_hi")
FAR = ("y_lo", "z")
VMEM_LIMIT = 14 << 20
SPLIT = (2, 8, 4, 2, 2)
STEP_TILES = 1


def sent(value, target):
    count = lax.axis_size(AXES)
    return lax.ppermute(value, AXES, [(source, target(source, count)) for source in range(count)])


def to_core(value):
    return sent(value, lambda device, count: device ^ 1)


def to_row(value):
    return sent(value, lambda device, count: device ^ 2)


def is_long(first, second, count):
    half = count // GROUP // SPLIT[0]
    return first // GROUP // half != second // GROUP // half


def to_block(value, steps):
    count = lax.axis_size(AXES)
    pairs = [(source, (source + GROUP * steps) % count) for source in range(count)]
    return lax.ppermute(value, AXES, [pair for pair in pairs if not is_long(*pair, count)])


def to_long(value, turn):
    count = lax.axis_size(AXES)
    pairs = [
        (source, ((source + GROUP * steps) % count) ^ turn)
        for steps in (1, -1)
        for source in range(count)
    ]
    return lax.ppermute(value, AXES, [pair for pair in pairs if is_long(*pair, count)])


def to_all(value, axes):
    count = lax.axis_size(axes)
    copies = jnp.broadcast_to(value[None], (count,) + value.shape)
    return lax.all_to_all(copies, axes, 0, 0, tiled=True)


def gelu_parts(pre_act):
    inner = 0.7978845608028654 * (pre_act + 0.044715 * pre_act * pre_act * pre_act)
    tangent = jnp.tanh(inner)
    value_part = 0.5 * pre_act * (1.0 + tangent)
    slope = 0.5 * (1.0 + tangent) + 0.5 * pre_act * (
        1.0 - tangent * tangent
    ) * 0.7978845608028654 * (1.0 + 0.134145 * pre_act * pre_act)
    return (value_part, slope)


def load_kernel(source_ref, held_ref, arrived):
    count = arrived.shape[0]
    rows = source_ref.shape[0] // count
    copies = [
        pltpu.make_async_copy(
            source_ref.at[pl.ds(i * rows, rows)], held_ref.at[pl.ds(i * rows, rows)], arrived.at[i]
        )
        for i in range(count)
    ]
    for copy in copies:
        copy.start()
    for copy in copies:
        copy.wait()


def turned(refs, index):
    terms = [ref[index].astype(jnp.float32) for ref in refs]
    return jnp.swapaxes(sum(terms[1:], terms[0]), 0, 1)


def merge_kernel(keep_ref, core_ref, up_ref, down_ref, long_ref, out_ref):
    refs = (keep_ref.at[1, 1], core_ref.at[1, 1], up_ref.at[1], down_ref.at[1], long_ref.at[1])
    for tile in range(PIECE_TILES):
        out_ref[tile * TILE : (tile + 1) * TILE, :] = turned(refs, tile).astype(jnp.bfloat16)


def final_kernel(keep_ref, core_ref, up_ref, down_ref, long_ref, last_ref, out_ref):
    refs = (keep_ref.at[1, 0], core_ref.at[1, 0], up_ref.at[0], down_ref.at[0], long_ref.at[0])
    count = out_ref.shape[0] // TILE
    for sub in range(count):
        tile = pl.program_id(0) * count + sub
        rows = pl.ds(pl.multiple_of(tile * TILE, TILE), TILE)
        total = turned(refs, tile) + last_ref[rows, :].astype(jnp.float32)
        out_ref[sub * TILE : (sub + 1) * TILE, :] = total


def forward_kernel(
    factor, place_ref, core_ref, window_ref, values_ref, grad_ref, weight_ref, bias_ref,
    act_ref, back_ref, own_ref, other_ref, agg_ref, pre_ref, bias_sum_ref,
):
    step = pl.program_id(0)
    weight = weight_ref[...]
    for sub in range(STEP_TILES):
        rows = slice(sub * TILE, (sub + 1) * TILE)
        tile = step * STEP_TILES + sub
        place = pl.ds(pl.multiple_of(tile * TILE, TILE), TILE)
        total = None
        for pair in range(SLOTS // 2):
            one = window_ref[place_ref[tile, 2 * pair]]
            two = window_ref[place_ref[tile, 2 * pair + 1]]
            term = jnp.dot(
                values_ref[place, 2 * pair * TILE : (2 * pair + 2) * TILE],
                jnp.concatenate([one, two], axis=0),
                preferred_element_type=jnp.float32,
            )
            total = term if total is None else total + term
        aggregated = total.astype(jnp.bfloat16)
        pre_act = jnp.dot(aggregated, weight, preferred_element_type=jnp.float32) + bias_ref[...]
        value_part, slope = gelu_parts(pre_act)
        act_ref[rows, :] = value_part.astype(jnp.bfloat16)
        pre_wide = (grad_ref[rows, :].astype(jnp.float32) * slope).astype(jnp.bfloat16)
        back_ref[tile] = lax.dot_general(
            weight, pre_wide, (((1,), (1,)), ((), ())), preferred_element_type=jnp.float32
        ).astype(jnp.bfloat16)
        agg_ref[place, :] = aggregated
        pre_ref[place, :] = pre_wide
        part = jnp.sum(pre_wide.astype(jnp.float32).reshape(TILE // 8, 8, -1), axis=0)
        bias_sum_ref[pl.ds(pl.multiple_of(tile * 8, 8), 8), :] = part

    @pl.when(step == pl.num_programs(0) - 1)
    def _():
        sums = factor * lax.dot_general(
            agg_ref[...], pre_ref[...], (((0,), (0,)), ((), ())), preferred_element_type=jnp.float32
        )
        bias_sum = jnp.sum(bias_sum_ref[...], axis=0, keepdims=True) * factor
        count, rows_of, _ = own_ref.shape
        out_dim = sums.shape[1]
        parts = [bias_sum[:, i * TILE : (i + 1) * TILE] for i in range(out_dim // TILE)]
        parts.append(jnp.zeros((rows_of - len(parts), TILE), jnp.float32))
        side = jnp.concatenate(parts, axis=0)
        for turn, sums_ref in enumerate((own_ref, other_ref)):
            core = jnp.bitwise_xor(core_ref[0], turn)
            for chunk in range(count):
                low = sums[2 * chunk * rows_of : (2 * chunk + 1) * rows_of]
                high = sums[(2 * chunk + 1) * rows_of : (2 * chunk + 2) * rows_of]
                sums_ref[chunk, :, :out_dim] = jnp.where(core == 0, low, high)
                sums_ref[chunk, :, out_dim:] = side


def backward_kernel(
    place_ref, back_ref, values_ref, keep_ref, send_ref, total_ref
):
    step = pl.program_id(0)

    @pl.when(step == 0)
    def _():
        total_ref[...] = jnp.zeros_like(total_ref)

    for sub in range(STEP_TILES):
        tile = step * STEP_TILES + sub
        back = back_ref[tile]
        place = pl.ds(pl.multiple_of(tile * TILE, TILE), TILE)
        for pair in range(SLOTS // 2):
            term = jnp.dot(
                back,
                values_ref[place, 2 * pair * TILE : (2 * pair + 2) * TILE],
                preferred_element_type=jnp.float32,
            )
            for half in range(2):
                spot = place_ref[step * STEP_TILES + sub, 2 * pair + half]
                total_ref[spot] += term[:, half * TILE : (half + 1) * TILE]

    @pl.when(step == pl.num_programs(0) - 1)
    def _():
        half = DUMMY // 2
        keep_ref[...] = total_ref[:half].astype(jnp.bfloat16)
        send_ref[...] = total_ref[half : 2 * half].astype(jnp.bfloat16)


def layer(features, weight, bias, tile_values, tile_cols, tile_counts, out_grad):
    rows_dev, in_dim = features.shape
    out_dim = weight.shape[1]
    row_tiles = rows_dev // TILE
    nodes = rows_dev * lax.axis_size(AXES)
    factor = 1.0 / math.sqrt(nodes)
    rep = lax.axis_index(("y_hi", "core"))
    core = lax.axis_index("core")
    chunks = lax.axis_size(NEAR)
    chunk_rows = in_dim // (2 * chunks)
    step_rows = STEP_TILES * TILE

    block = lax.axis_index(("y_lo", "z", "x"))
    half_blocks = lax.axis_size(("z", "x"))
    is_ends = {-1: block % half_blocks == 0, 1: block % half_blocks == half_blocks - 1}
    other_row = to_row(features)
    pieces = {0: (features, other_row)}
    direct = {}
    for steps in (1, -1):
        direct[steps] = to_block(features, steps)
    long_one = to_long(features, 0)
    long_two = to_long(features, 2)
    for steps in (1, -1):
        crossed = to_block(other_row, steps)
        pieces[-steps] = (
            jnp.where(is_ends[-steps], long_one, direct[steps]),
            jnp.where(is_ends[-steps], long_two, crossed),
        )
    near = [piece for offset in (-1, 0, 1) for piece in pieces[offset]]
    far = [to_core(piece) for piece in near]
    blank = jnp.zeros_like(features)
    window = jnp.stack(near + far + [blank]).reshape(-1, TILE, in_dim)

    block_tile = tile_cols % (GROUP * PIECE_TILES)
    offset = tile_cols // (GROUP * PIECE_TILES)
    turn = (block_tile // PIECE_TILES) ^ rep
    place = ((turn & 1) * (PIECES // 2) + offset * 2 + (turn >> 1)) * PIECE_TILES
    place = place + block_tile % PIECE_TILES
    is_live = jnp.arange(SLOTS)[None, :] < tile_counts[:, None]
    place = jnp.where(is_live, place, DUMMY).astype(jnp.int32)

    load = pl.pallas_call(
        load_kernel,
        out_shape=pltpu.VMEM(tile_values.shape, tile_values.dtype),
        in_specs=[pl.BlockSpec(memory_space=pltpu.HBM)],
        out_specs=pl.BlockSpec(memory_space=pltpu.VMEM),
        scratch_shapes=[pltpu.SemaphoreType.DMA((row_tiles,))],
        compiler_params=pltpu.CompilerParams(vmem_limit_bytes=1 << 20),
        cost_estimate=pl.CostEstimate(flops=0, bytes_accessed=16 << 20, transcendentals=0),
        name="load",
    )
    tile_values = load(pltpu.with_memory_space_constraint(tile_values, pltpu.HBM))
    whole = pl.BlockSpec(memory_space=pltpu.VMEM)
    act, back, own_sums, other_sums = pl.pallas_call(
        functools.partial(forward_kernel, factor),
        out_shape=(
            jax.ShapeDtypeStruct((rows_dev, out_dim), jnp.bfloat16),
            jax.ShapeDtypeStruct((row_tiles, in_dim, TILE), jnp.bfloat16),
            jax.ShapeDtypeStruct((chunks, chunk_rows, out_dim + TILE), jnp.float32),
            jax.ShapeDtypeStruct((chunks, chunk_rows, out_dim + TILE), jnp.float32),
        ),
        grid_spec=pltpu.PrefetchScalarGridSpec(
            num_scalar_prefetch=2,
            grid=(row_tiles // STEP_TILES,),
            in_specs=[
                whole,
                whole,
                pl.BlockSpec((step_rows, out_dim), lambda i, *_: (i, 0)),
                whole,
                whole,
            ],
            out_specs=(
                pl.BlockSpec((step_rows, out_dim), lambda i, *_: (i, 0)),
                whole,
                whole,
                whole,
            ),
            scratch_shapes=[
                pltpu.VMEM((rows_dev, in_dim), jnp.bfloat16),
                pltpu.VMEM((rows_dev, out_dim), jnp.bfloat16),
                pltpu.VMEM((row_tiles * 8, out_dim), jnp.float32),
            ],
        ),
        compiler_params=pltpu.CompilerParams(vmem_limit_bytes=VMEM_LIMIT),
        cost_estimate=pl.CostEstimate(flops=3 << 30, bytes_accessed=15 << 20, transcendentals=1 << 19),
        name="forward",
    )(place, core.reshape(1).astype(jnp.int32), window, tile_values, out_grad, weight, bias.reshape(1, -1))

    half_tiles = DUMMY // 2
    backward = pl.pallas_call(
        backward_kernel,
        out_shape=(jax.ShapeDtypeStruct((half_tiles, in_dim, TILE), jnp.bfloat16),) * 2,
        grid_spec=pltpu.PrefetchScalarGridSpec(
            num_scalar_prefetch=1,
            grid=(row_tiles // STEP_TILES,),
            in_specs=[
                whole,
                whole,
            ],
            out_specs=(whole,) * 2,
            scratch_shapes=[pltpu.VMEM((DUMMY + 1, in_dim, TILE), jnp.float32)],
        ),
        compiler_params=pltpu.CompilerParams(vmem_limit_bytes=VMEM_LIMIT),
        cost_estimate=pl.CostEstimate(flops=2 << 30, bytes_accessed=12 << 20, transcendentals=0),
        name="backward",
    )
    keep, send = backward(place, back, tile_values)

    wide = lambda value: value.astype(jnp.float32)
    moved_sums = to_core(other_sums)
    part = own_sums + moved_sums
    from_core = to_core(send)
    part = jnp.sum(lax.all_to_all(part, NEAR, 0, 0, tiled=True), axis=0)
    part, from_core = lax.optimization_barrier((part, from_core))
    keep, from_core = (value.reshape(3, 2, -1, in_dim, TILE) for value in (keep, from_core))
    moved, terms = [], {}
    for steps in (1, -1):
        terms[steps] = (wide(keep[1 + steps]) + wide(from_core[1 + steps])).astype(jnp.bfloat16)
        moved.append(to_block(terms[steps], steps))
    moved.append(to_long(jnp.where(is_ends[-1], terms[-1], terms[1]), 0))
    part = to_all(part, FAR)
    part = jnp.sum(part, axis=0)
    bias_grad = part[: out_dim // TILE, out_dim:].reshape(out_dim)
    operands = (keep, from_core, *moved)
    other = pl.pallas_call(
        merge_kernel,
        out_shape=jax.ShapeDtypeStruct((rows_dev, in_dim), jnp.bfloat16),
        in_specs=[whole] * 5,
        out_specs=whole,
        compiler_params=pltpu.CompilerParams(vmem_limit_bytes=6 << 20),
        cost_estimate=pl.CostEstimate(flops=1 << 20, bytes_accessed=2 << 20, transcendentals=0),
        name="merge",
    )(*operands)
    last = to_row(other)
    mine = to_all(part[:, :out_dim], (*NEAR, "core"))
    weight_grad = mine.reshape(in_dim, out_dim)
    final_tiles = 2
    rows_spec = pl.BlockSpec((final_tiles * TILE, in_dim), lambda i: (i, 0))
    final = pl.pallas_call(
        final_kernel,
        out_shape=jax.ShapeDtypeStruct((rows_dev, in_dim), jnp.float32),
        grid=(PIECE_TILES // final_tiles,),
        in_specs=[whole] * 6,
        out_specs=rows_spec,
        compiler_params=pltpu.CompilerParams(vmem_limit_bytes=6 << 20),
        cost_estimate=pl.CostEstimate(flops=1 << 20, bytes_accessed=2 << 20, transcendentals=0),
        name="final",
    )
    feature_grad = final(*operands, last)
    return (act, feature_grad, weight_grad, bias_grad)


def solution(mesh):
    mesh = jax.sharding.Mesh(mesh.devices.reshape(SPLIT), AXES)
    in_specs = (
        P(AXES, None),
        P(),
        P(),
        P(AXES, None),
        P(AXES, None),
        P(AXES),
        P(AXES, None),
    )
    out_specs = (P(AXES, None), P(AXES, None), P(), P())
    return jax.shard_map(layer, mesh=mesh, in_specs=in_specs, out_specs=out_specs, check_vma=False)
```

```python
import functools
import math

import jax
import jax.numpy as jnp
from jax import lax
from jax.experimental import pallas as pl
from jax.experimental.pallas import tpu as pltpu
from jax.sharding import PartitionSpec as P


TILE = 128
REACH = 1
SLOTS = 32
GROUP = 4
PIECE_TILES = 8
PIECES = (2 * REACH + 1) * GROUP
DUMMY = PIECES * PIECE_TILES
AXES = ("y_lo", "z", "x", "y_hi", "core")
NEAR = ("x", "y_hi")
FAR = ("y_lo", "z")
VMEM_LIMIT = 14 << 20
SPLIT = (2, 8, 4, 2, 2)
AHEAD = 3
STEP_TILES = 1


def sent(value, target):
    count = lax.axis_size(AXES)
    return lax.ppermute(value, AXES, [(source, target(source, count)) for source in range(count)])


def to_core(value):
    return sent(value, lambda device, count: device ^ 1)


def to_row(value):
    return sent(value, lambda device, count: device ^ 2)


def to_block(value, steps):
    return sent(value, lambda device, count: (device + GROUP * steps) % count)


def to_all(value, axes):
    count = lax.axis_size(axes)
    copies = jnp.broadcast_to(value[None], (count,) + value.shape)
    return lax.all_to_all(copies, axes, 0, 0, tiled=True)


def gelu_parts(pre_act):
    inner = 0.7978845608028654 * (pre_act + 0.044715 * pre_act * pre_act * pre_act)
    tangent = jnp.tanh(inner)
    value_part = 0.5 * pre_act * (1.0 + tangent)
    slope = 0.5 * (1.0 + tangent) + 0.5 * pre_act * (
        1.0 - tangent * tangent
    ) * 0.7978845608028654 * (1.0 + 0.134145 * pre_act * pre_act)
    return (value_part, slope)


def load_kernel(source_ref, held_ref, arrived):
    count = arrived.shape[0]
    rows = source_ref.shape[0] // count
    copies = [
        pltpu.make_async_copy(
            source_ref.at[pl.ds(i * rows, rows)], held_ref.at[pl.ds(i * rows, rows)], arrived.at[i]
        )
        for i in range(count)
    ]
    for copy in copies:
        copy.start()
    for copy in copies:
        copy.wait()


def turned(refs, index):
    terms = [ref[index].astype(jnp.float32) for ref in refs]
    return jnp.swapaxes(terms[0] + terms[1] + terms[2] + terms[3], 0, 1)


def merge_kernel(keep_ref, core_ref, up_ref, down_ref, out_ref):
    refs = (keep_ref.at[1, 1], core_ref.at[1, 1], up_ref.at[1], down_ref.at[1])
    for tile in range(PIECE_TILES):
        out_ref[tile * TILE : (tile + 1) * TILE, :] = turned(refs, tile).astype(jnp.bfloat16)


def final_kernel(keep_ref, core_ref, up_ref, down_ref, last_ref, out_ref):
    refs = (keep_ref.at[1, 0], core_ref.at[1, 0], up_ref.at[0], down_ref.at[0])
    count = out_ref.shape[0] // TILE
    for sub in range(count):
        tile = pl.program_id(0) * count + sub
        rows = pl.ds(pl.multiple_of(tile * TILE, TILE), TILE)
        total = turned(refs, tile) + last_ref[rows, :].astype(jnp.float32)
        out_ref[sub * TILE : (sub + 1) * TILE, :] = total


def forward_kernel(
    factor, place_ref, core_ref, window_ref, values_ref, grad_ref, weight_ref, bias_ref,
    act_ref, back_ref, own_ref, other_ref, agg_ref, pre_ref, bias_sum_ref,
):
    step = pl.program_id(0)
    weight = weight_ref[...]
    for sub in range(STEP_TILES):
        rows = slice(sub * TILE, (sub + 1) * TILE)
        tile = step * STEP_TILES + sub
        place = pl.ds(pl.multiple_of(tile * TILE, TILE), TILE)
        total = None
        for pair in range(SLOTS // 2):
            one = window_ref[place_ref[tile, 2 * pair]]
            two = window_ref[place_ref[tile, 2 * pair + 1]]
            term = jnp.dot(
                values_ref[place, 2 * pair * TILE : (2 * pair + 2) * TILE],
                jnp.concatenate([one, two], axis=0),
                preferred_element_type=jnp.float32,
            )
            total = term if total is None else total + term
        aggregated = total.astype(jnp.bfloat16)
        pre_act = jnp.dot(aggregated, weight, preferred_element_type=jnp.float32) + bias_ref[...]
        value_part, slope = gelu_parts(pre_act)
        act_ref[rows, :] = value_part.astype(jnp.bfloat16)
        pre_wide = (grad_ref[rows, :].astype(jnp.float32) * slope).astype(jnp.bfloat16)
        back_ref[tile] = lax.dot_general(
            weight, pre_wide, (((1,), (1,)), ((), ())), preferred_element_type=jnp.float32
        ).astype(jnp.bfloat16)
        agg_ref[place, :] = aggregated
        pre_ref[place, :] = pre_wide
        part = jnp.sum(pre_wide.astype(jnp.float32).reshape(TILE // 8, 8, -1), axis=0)
        bias_sum_ref[pl.ds(pl.multiple_of(tile * 8, 8), 8), :] = part

    @pl.when(step == pl.num_programs(0) - 1)
    def _():
        sums = factor * lax.dot_general(
            agg_ref[...], pre_ref[...], (((0,), (0,)), ((), ())), preferred_element_type=jnp.float32
        )
        bias_sum = jnp.sum(bias_sum_ref[...], axis=0, keepdims=True) * factor
        count, rows_of, _ = own_ref.shape
        out_dim = sums.shape[1]
        parts = [bias_sum[:, i * TILE : (i + 1) * TILE] for i in range(out_dim // TILE)]
        parts.append(jnp.zeros((rows_of - len(parts), TILE), jnp.float32))
        side = jnp.concatenate(parts, axis=0)
        for turn, sums_ref in enumerate((own_ref, other_ref)):
            core = jnp.bitwise_xor(core_ref[0], turn)
            for chunk in range(count):
                low = sums[2 * chunk * rows_of : (2 * chunk + 1) * rows_of]
                high = sums[(2 * chunk + 1) * rows_of : (2 * chunk + 2) * rows_of]
                sums_ref[chunk, :, :out_dim] = jnp.where(core == 0, low, high)
                sums_ref[chunk, :, out_dim:] = side


def backward_kernel(
    place_ref, back_ref, source_ref, keep_ref, send_ref, total_ref, held_ref, arrived
):
    step = pl.program_id(0)
    count = held_ref.shape[0]

    def copy(tile):
        rows = pl.ds(pl.multiple_of(tile * TILE, TILE), TILE)
        return pltpu.make_async_copy(source_ref.at[rows], held_ref.at[tile], arrived.at[tile])

    @pl.when(step == 0)
    def _():
        for tile in range(AHEAD):
            copy(tile).start()
        total_ref[...] = jnp.zeros_like(total_ref)

    @pl.when(step + AHEAD < count)
    def _():
        copy(step + AHEAD).start()

    copy(step).wait()
    back = back_ref[step]
    for pair in range(SLOTS // 2):
        term = jnp.dot(
            back,
            held_ref[step, :, 2 * pair * TILE : (2 * pair + 2) * TILE],
            preferred_element_type=jnp.float32,
        )
        for half in range(2):
            spot = place_ref[step, 2 * pair + half]
            total_ref[spot] += term[:, half * TILE : (half + 1) * TILE]

    @pl.when(step == pl.num_programs(0) - 1)
    def _():
        half = DUMMY // 2
        keep_ref[...] = total_ref[:half].astype(jnp.bfloat16)
        send_ref[...] = total_ref[half : 2 * half].astype(jnp.bfloat16)


def layer(features, weight, bias, tile_values, tile_cols, tile_counts, out_grad):
    rows_dev, in_dim = features.shape
    out_dim = weight.shape[1]
    row_tiles = rows_dev // TILE
    nodes = rows_dev * lax.axis_size(AXES)
    factor = 1.0 / math.sqrt(nodes)
    rep = lax.axis_index(("y_hi", "core"))
    core = lax.axis_index("core")
    chunks = lax.axis_size(NEAR)
    chunk_rows = in_dim // (2 * chunks)
    step_rows = STEP_TILES * TILE

    other_row = to_row(features)
    pieces = {0: (features, other_row)}
    for steps in (1, -1):
        near = to_block(features, steps)
        far = to_block(other_row, steps)
        pieces[-steps] = (near, far)
    near = [piece for offset in (-1, 0, 1) for piece in pieces[offset]]
    far = [to_core(piece) for piece in near]
    blank = jnp.zeros_like(features)
    window = jnp.stack(near + far + [blank]).reshape(-1, TILE, in_dim)

    block_tile = tile_cols % (GROUP * PIECE_TILES)
    offset = tile_cols // (GROUP * PIECE_TILES)
    turn = (block_tile // PIECE_TILES) ^ rep
    place = ((turn & 1) * (PIECES // 2) + offset * 2 + (turn >> 1)) * PIECE_TILES
    place = place + block_tile % PIECE_TILES
    is_live = jnp.arange(SLOTS)[None, :] < tile_counts[:, None]
    place = jnp.where(is_live, place, DUMMY).astype(jnp.int32)

    load = pl.pallas_call(
        load_kernel,
        out_shape=pltpu.VMEM(tile_values.shape, tile_values.dtype),
        in_specs=[pl.BlockSpec(memory_space=pltpu.HBM)],
        out_specs=pl.BlockSpec(memory_space=pltpu.VMEM),
        scratch_shapes=[pltpu.SemaphoreType.DMA((row_tiles,))],
        compiler_params=pltpu.CompilerParams(vmem_limit_bytes=1 << 20),
        cost_estimate=pl.CostEstimate(flops=0, bytes_accessed=16 << 20, transcendentals=0),
        name="load",
    )
    tile_values = pltpu.with_memory_space_constraint(tile_values, pltpu.HBM)
    near_values = load(tile_values)
    whole = pl.BlockSpec(memory_space=pltpu.VMEM)
    act, back, own_sums, other_sums = pl.pallas_call(
        functools.partial(forward_kernel, factor),
        out_shape=(
            jax.ShapeDtypeStruct((rows_dev, out_dim), jnp.bfloat16),
            jax.ShapeDtypeStruct((row_tiles, in_dim, TILE), jnp.bfloat16),
            jax.ShapeDtypeStruct((chunks, chunk_rows, out_dim + TILE), jnp.float32),
            jax.ShapeDtypeStruct((chunks, chunk_rows, out_dim + TILE), jnp.float32),
        ),
        grid_spec=pltpu.PrefetchScalarGridSpec(
            num_scalar_prefetch=2,
            grid=(row_tiles // STEP_TILES,),
            in_specs=[
                whole,
                whole,
                pl.BlockSpec((step_rows, out_dim), lambda i, *_: (i, 0)),
                whole,
                whole,
            ],
            out_specs=(
                pl.BlockSpec((step_rows, out_dim), lambda i, *_: (i, 0)),
                whole,
                whole,
                whole,
            ),
            scratch_shapes=[
                pltpu.VMEM((rows_dev, in_dim), jnp.bfloat16),
                pltpu.VMEM((rows_dev, out_dim), jnp.bfloat16),
                pltpu.VMEM((row_tiles * 8, out_dim), jnp.float32),
            ],
        ),
        compiler_params=pltpu.CompilerParams(vmem_limit_bytes=VMEM_LIMIT),
        cost_estimate=pl.CostEstimate(flops=3 << 30, bytes_accessed=15 << 20, transcendentals=1 << 19),
        name="forward",
    )(place, core.reshape(1).astype(jnp.int32), window, near_values, out_grad, weight, bias.reshape(1, -1))

    half_tiles = DUMMY // 2
    backward = pl.pallas_call(
        backward_kernel,
        out_shape=(jax.ShapeDtypeStruct((half_tiles, in_dim, TILE), jnp.bfloat16),) * 2,
        grid_spec=pltpu.PrefetchScalarGridSpec(
            num_scalar_prefetch=1,
            grid=(row_tiles,),
            in_specs=[
                whole,
                pl.BlockSpec(memory_space=pltpu.HBM),
            ],
            out_specs=(whole,) * 2,
            scratch_shapes=[
                pltpu.VMEM((DUMMY + 1, in_dim, TILE), jnp.float32),
                pltpu.VMEM((row_tiles, TILE, SLOTS * TILE), jnp.bfloat16),
                pltpu.SemaphoreType.DMA((row_tiles,)),
            ],
        ),
        compiler_params=pltpu.CompilerParams(vmem_limit_bytes=20 << 20),
        cost_estimate=pl.CostEstimate(flops=2 << 30, bytes_accessed=12 << 20, transcendentals=0),
        name="backward",
    )
    keep, send = backward(place, back, tile_values)

    wide = lambda value: value.astype(jnp.float32)
    moved_sums = to_core(other_sums)
    part = own_sums + moved_sums
    from_core = to_core(send)
    part = lax.all_to_all(part, NEAR, 0, 0, tiled=True)
    part = jnp.sum(part, axis=0)
    keep, from_core = (value.reshape(3, 2, -1, in_dim, TILE) for value in (keep, from_core))
    moved = []
    for steps in (1, -1):
        term = wide(keep[1 + steps]) + wide(from_core[1 + steps])
        moved.append(to_block(term.astype(jnp.bfloat16), steps))
    part = to_all(part, FAR)
    part = jnp.sum(part, axis=0)
    bias_grad = part[: out_dim // TILE, out_dim:].reshape(out_dim)
    operands = (keep, from_core, moved[0], moved[1])
    merge = pl.pallas_call(
        merge_kernel,
        out_shape=jax.ShapeDtypeStruct((rows_dev, in_dim), jnp.bfloat16),
        in_specs=[whole] * 4,
        out_specs=whole,
        compiler_params=pltpu.CompilerParams(vmem_limit_bytes=6 << 20),
        cost_estimate=pl.CostEstimate(flops=1 << 20, bytes_accessed=2 << 20, transcendentals=0),
        name="merge",
    )
    other = merge(*operands)
    last = to_row(other)
    mine = to_all(part[:, :out_dim], NEAR)
    theirs = to_core(mine)
    odd = core == 1
    weight_grad = jnp.stack([jnp.where(odd, theirs, mine), jnp.where(odd, mine, theirs)], axis=1)
    weight_grad = weight_grad.reshape(in_dim, out_dim)
    final_tiles = 2
    rows_spec = pl.BlockSpec((final_tiles * TILE, in_dim), lambda i: (i, 0))
    final = pl.pallas_call(
        final_kernel,
        out_shape=jax.ShapeDtypeStruct((rows_dev, in_dim), jnp.float32),
        grid=(PIECE_TILES // final_tiles,),
        in_specs=[whole] * 5,
        out_specs=rows_spec,
        compiler_params=pltpu.CompilerParams(vmem_limit_bytes=6 << 20),
        cost_estimate=pl.CostEstimate(flops=1 << 20, bytes_accessed=2 << 20, transcendentals=0),
        name="final",
    )
    feature_grad = final(*operands, last)
    return (act, feature_grad, weight_grad, bias_grad)


def solution(mesh):
    mesh = jax.sharding.Mesh(mesh.devices.reshape(SPLIT), AXES)
    in_specs = (
        P(AXES, None),
        P(),
        P(),
        P(AXES, None),
        P(AXES, None),
        P(AXES),
        P(AXES, None),
    )
    out_specs = (P(AXES, None), P(AXES, None), P(), P())
    return jax.shard_map(layer, mesh=mesh, in_specs=in_specs, out_specs=out_specs, check_vma=False)
```
